256 devices in a mesh: seq: 64 (over y, z, core), head: 4 (over x).
Axes of the slice: x: 4, y: 4, z: 8, core: 2. Of those that a mesh axis runs over, the one named last changes fastest.
Arguments:
- queries: bfloat16 [16384, 8, 1024], P('seq', 'head')
- keys: bfloat16 [16384, 8, 128], P('seq', 'head')
- values: bfloat16 [16384, 8, 128], P('seq', 'head'), may hold values from -6 to 6
- retrieval_ids: int32 [4], replicated, may hold values from 0 to 7, as said below
- vertical_blocks: int32 [128, 8, 16], P('seq'), may hold values from 0 to 127, as said below
- slash_offsets: int32 [128, 8, 16], P('seq'), may hold values from 0 to 127, as said below
- sink_blocks: int32 [8], replicated, may hold values from 1 to 2
- window_blocks: int32 [8], replicated, may hold values from 1 to 5
Outputs:
- attended: bfloat16 [16384, 8, 1024], P('seq', 'head')
The draws below stay inside these ranges and needn't reach their ends.
Inputs may be any that keep to these rules, and one draw needn't show every extreme that they name: `retrieval_ids`: 4 different KV head numbers in increasing order. `vertical_blocks`: each entry is at most the index of its query block (dimension 0). `slash_offsets`: each entry is at most the index of its query block (dimension 0).
All inputs are finite; a program needn't handle non-finite values.
Results may differ from the reference program's by a relative error of at most 0.0044.
Values may be sent and summed in bfloat16 or wider, within the bound.
A program may use at most 128 MiB of HBM per device.

```python
import jax
import jax.numpy as jnp
from jax import lax

KV_HEADS = 8
GROUP = 8
HEAD_DIM = 128
BLOCK = 128
VERT = 16
SLASH = 16
RETR = 4
SINK_MAX = 2
WIN_MAX = 5
TOKENS = 16384
QBLOCKS = 128


def pick_retrieval(key):
    order = jax.random.permutation(jax.random.fold_in(key, 101), KV_HEADS)
    return jnp.sort(order[:RETR]).astype(jnp.int32)


def running_pick(key, salt):
    chosen_ids = pick_retrieval(key)
    flags = jnp.any(jnp.arange(KV_HEADS)[:, None] == chosen_ids[None, :], axis=1).astype(jnp.int32)
    order = jax.random.permutation(jax.random.fold_in(key, salt), KV_HEADS)
    ranking = jnp.arange(KV_HEADS, dtype=jnp.int32) + KV_HEADS * flags[order]
    return order[jnp.argmin(ranking)]


def draw_retrieval_ids(key, part):
    return pick_retrieval(key)


def draw_window_blocks(key, part):
    base_draw = jax.random.randint(jax.random.fold_in(key, 201), (KV_HEADS,), 1, WIN_MAX + 1)
    widest = running_pick(key, 202)
    return jnp.where(jnp.arange(KV_HEADS) == widest, WIN_MAX, base_draw).astype(jnp.int32)


def draw_sink_blocks(key, part):
    base_draw = jax.random.randint(jax.random.fold_in(key, 301), (KV_HEADS,), 1, SINK_MAX + 1)
    widest = running_pick(key, 302)
    return jnp.where(jnp.arange(KV_HEADS) == widest, SINK_MAX, base_draw).astype(jnp.int32)


def draw_vertical_blocks(key, part):
    upper = jnp.arange(QBLOCKS, dtype=jnp.int32)[:, None, None] + 1
    return jax.random.randint(jax.random.fold_in(key, 401), (QBLOCKS, KV_HEADS, VERT), 0, upper).astype(jnp.int32)


def draw_slash_offsets(key, part):
    upper = jnp.arange(QBLOCKS, dtype=jnp.int32)[:, None, None] + 1
    return jax.random.randint(jax.random.fold_in(key, 501), (QBLOCKS, KV_HEADS, SLASH), 0, upper).astype(jnp.int32)


def draw_queries(key, part):
    base_draw = jax.random.normal(jax.random.fold_in(key, 601), (TOKENS, KV_HEADS, GROUP * HEAD_DIM), jnp.float32)
    return base_draw.astype(jnp.bfloat16)


def draw_keys(key, part):
    base_draw = jax.random.normal(jax.random.fold_in(key, 611), (TOKENS, KV_HEADS, HEAD_DIM), jnp.float32)
    return base_draw.astype(jnp.bfloat16)


def levels(key, shape, shards, least, largest):
    def one(dim, parts):
        steps = jax.random.uniform(jax.random.fold_in(jax.random.fold_in(key, 6), dim), (parts,), jnp.float32, least / len(shards), largest / len(shards))
        return jnp.repeat(jnp.exp(steps), shape[dim] // parts).reshape((-1,) + (1,) * (len(shape) - dim - 1))

    loudness = one(*shards[0])
    for cut in shards[1:]:
        loudness = loudness * one(*cut)
    return loudness


def normal_values(rng, extent, scale, bound, shards=(), kind=jnp.bfloat16):
    factor_of = levels(rng, extent, shards, -0.22, 0.18) if shards else 1.0
    values = jax.random.normal(rng, extent, jnp.float32) * scale * factor_of
    return jnp.minimum(jnp.maximum(values, -bound), bound).astype(kind)


def setup_inputs(seed: int = 0) -> dict:
    key_of = jax.random.split(jax.random.key(seed), 9)
    queries = draw_queries(jax.random.fold_in(key_of[8], 71), 0)
    keys = draw_keys(jax.random.fold_in(key_of[8], 71), 0)
    values = normal_values(key_of[2], (TOKENS, KV_HEADS, HEAD_DIM), 1.0, 6.0, ((0, 64), (1, 4)))
    retrieval_ids = draw_retrieval_ids(jax.random.fold_in(key_of[8], 71), 0)
    vertical_blocks = draw_vertical_blocks(jax.random.fold_in(key_of[8], 71), 0)
    slash_offsets = draw_slash_offsets(jax.random.fold_in(key_of[8], 71), 0)
    sink_blocks = draw_sink_blocks(jax.random.fold_in(key_of[8], 71), 0)
    window_blocks = draw_window_blocks(jax.random.fold_in(key_of[8], 71), 0)
    return {"queries": queries, "keys": keys, "values": values, "retrieval_ids": retrieval_ids, "vertical_blocks": vertical_blocks, "slash_offsets": slash_offsets, "sink_blocks": sink_blocks, "window_blocks": window_blocks}


masked_score = -1.0e30


def candidate_blocks(head_id, query_block, is_retrieval, vertical_blocks, slash_offsets, sink_blocks, window_blocks):
    listed = jnp.concatenate([
        jnp.reshape(query_block, (1,)).astype(jnp.int32),
        vertical_blocks[query_block, head_id].astype(jnp.int32),
        (query_block - slash_offsets[query_block, head_id]).astype(jnp.int32)])
    width_all = listed.shape[0]
    earlier = jnp.arange(width_all)[:, None] > jnp.arange(width_all)[None, :]
    repeated = jnp.any(earlier & (listed[:, None] == listed[None, :]), axis=1)
    listed_ok = jnp.logical_not(repeated) & (listed <= query_block) & (listed >= 0)
    sink_ids = jnp.arange(SINK_MAX, dtype=jnp.int32)
    window_ids = (query_block - jnp.arange(WIN_MAX, dtype=jnp.int32)).astype(jnp.int32)
    sink_ok = (sink_ids < sink_blocks[head_id]) & (sink_ids <= query_block)
    window_ok = (window_ids > query_block - window_blocks[head_id]) & (window_ids >= sink_blocks[head_id]) & (window_ids >= 0)
    padding = width_all - SINK_MAX - WIN_MAX
    read = jnp.concatenate([sink_ids, window_ids, jnp.zeros((padding,), jnp.int32)])
    read_ok = jnp.concatenate([sink_ok, window_ok, jnp.zeros((padding,), bool)])
    chosen = jnp.where(is_retrieval, listed, read)
    usable = jnp.where(is_retrieval, listed_ok, read_ok)
    return chosen, usable


def reference(queries, keys, values, retrieval_ids, vertical_blocks, slash_offsets, sink_blocks, window_blocks):
    score_scale = HEAD_DIM ** -0.5
    key_tiles = keys.astype(jnp.float32).reshape(QBLOCKS, BLOCK, KV_HEADS, HEAD_DIM)
    value_tiles = values.astype(jnp.float32).reshape(QBLOCKS, BLOCK, KV_HEADS, HEAD_DIM)
    query_tiles = queries.astype(jnp.float32).reshape(QBLOCKS, BLOCK, KV_HEADS, GROUP, HEAD_DIM)
    retrieval_flags = jnp.any(jnp.arange(KV_HEADS, dtype=jnp.int32)[:, None] == retrieval_ids[None, :], axis=1)
    offsets = jnp.arange(BLOCK, dtype=jnp.int32)

    def per_head(head_id):
        is_retrieval = retrieval_flags[head_id]
        head_keys = jnp.take(key_tiles, head_id, axis=2)
        head_values = jnp.take(value_tiles, head_id, axis=2)
        head_queries = jnp.take(query_tiles, head_id, axis=2)

        def per_block(query_block):
            chosen, usable = candidate_blocks(head_id, query_block, is_retrieval, vertical_blocks, slash_offsets, sink_blocks, window_blocks)
            safe_ids = jnp.clip(chosen, 0, QBLOCKS - 1)
            key_rows = head_keys[safe_ids]
            value_rows = head_values[safe_ids]
            query_rows = head_queries[query_block]
            scores = jnp.einsum('tgd,csd->gtcs', query_rows, key_rows) * score_scale
            query_pos = query_block * BLOCK + offsets
            key_pos = chosen[:, None] * BLOCK + offsets[None, :]
            visible = usable[None, :, None] & (key_pos[None, :, :] <= query_pos[:, None, None])
            scores = jnp.where(visible[None], scores, masked_score)
            row_peak = jnp.max(scores, axis=(2, 3), keepdims=True)
            expo = jnp.exp(scores - row_peak)
            row_total = jnp.sum(expo, axis=(2, 3))
            rounded = lax.optimization_barrier(expo.astype(jnp.bfloat16)).astype(jnp.float32)
            mixed = jnp.einsum('gtcs,csd->tgd', rounded, value_rows) / jnp.transpose(row_total)[:, :, None]
            return mixed.reshape(BLOCK, GROUP * HEAD_DIM)

        return lax.map(per_block, jnp.arange(QBLOCKS, dtype=jnp.int32))

    result = lax.map(per_head, jnp.arange(KV_HEADS, dtype=jnp.int32))
    return jnp.transpose(result, (1, 2, 0, 3)).reshape(TOKENS, KV_HEADS, GROUP * HEAD_DIM).astype(jnp.bfloat16)
```

```python
import functools

import jax
import jax.numpy as jnp
from jax import lax
from jax.experimental import pallas as pl
from jax.experimental.pallas import tpu as pltpu
from jax.sharding import PartitionSpec as P

BLOCK=128; D=128; NEG=-1e30
LOG2E=1.4426950408889634

def attn_kernel(CH, RG, MODE, vert_ref, slash_ref, ids_ref, sink_ref, win_ref, pos_ref, q_ref, kv_ref, o_ref,
                kbuf, vbuf, sbuf, acc, stamp, cnt, sem):
    heads, toks, width = q_ref.shape
    G = width // D
    blocks_here = toks // BLOCK
    steps = heads * blocks_here
    first_block = pos_ref[0] * blocks_here
    first_head = pos_ref[1] * heads
    CB = CH // BLOCK
    rows = RG * BLOCK
    c2 = (D ** -0.5) * LOG2E

    def init(i, _):
        stamp[i] = -1
        return 0
    lax.fori_loop(0, 128, init, 0)
    vbuf[...] = jnp.zeros_like(vbuf)
    vbuf[:, :, D:] = jnp.ones((2, vbuf.shape[1], D), vbuf.dtype)
    kbuf[...] = jnp.zeros_like(kbuf)

    def copies(slot, h, c, n):
        src = kv_ref.at[c // 2, h]
        off = pl.multiple_of((c % 2) * BLOCK, BLOCK)
        dst = pl.multiple_of(n * BLOCK, BLOCK)
        return (pltpu.make_async_copy(src.at[0, pl.ds(off, BLOCK), :], kbuf.at[slot, pl.ds(dst, BLOCK), :], sem.at[slot]),
                pltpu.make_async_copy(src.at[1, pl.ds(off, BLOCK), :], vbuf.at[slot, pl.ds(dst, BLOCK), pl.ds(0, D)], sem.at[slot]))

    def fetch(step):
        slot = lax.rem(step, 2)
        h = step // blocks_here
        lb = lax.rem(step, blocks_here)
        head = first_head + h
        b = first_block + lb
        retr = (ids_ref[0] == head) | (ids_ref[1] == head) | (ids_ref[2] == head) | (ids_ref[3] == head)

        def add(c, ok, n):
            new = ok & (stamp[jnp.maximum(c, 0)] != step)
            @pl.when(new)
            def _():
                stamp[c] = step
                for cp in copies(slot, h, c, n):
                    cp.start()
            return n + new.astype(jnp.int32)

        n = add(b, True, jnp.int32(0))
        def retr_list(n):
            def one(j, n):
                n = add(vert_ref[lb, head, j], True, n)
                return add(b - slash_ref[lb, head, j], True, n)
            return lax.fori_loop(0, 16, one, n)
        def run_list(n):
            w = win_ref[head]; s = sink_ref[head]
            n = lax.fori_loop(0, jnp.minimum(s, b + 1), lambda c, n: add(c, True, n), n)
            return lax.fori_loop(1, jnp.minimum(w, b + 1), lambda d, n: add(b - d, True, n), n)
        n = lax.cond(retr, retr_list, run_list, n)
        cnt[slot] = n

    fetch(jnp.int32(0))

    def step_body(step, _):
        slot = lax.rem(step, 2)
        h = step // blocks_here
        lb = lax.rem(step, blocks_here)
        @pl.when(step + 1 < steps)
        def _():
            fetch(step + 1)
        n = cnt[slot]
        def wt(i, _):
            for cp in copies(slot, 0, 0, 0):
                cp.wait()
            return 0
        lax.fori_loop(0, n, wt, 0)
        row0 = pl.multiple_of(lb * BLOCK, BLOCK)
        chunks = (n + CB - 1) // CB
        def qrows(r):
            return jnp.concatenate([q_ref[h, pl.ds(row0, BLOCK), (r * RG + g) * D:(r * RG + g + 1) * D] for g in range(RG)], axis=0)
        NR = G // RG

        def scores(r, j, masked):
            off = pl.multiple_of(j * CH, CH)
            s = lax.dot_general(qrows(r), kbuf[slot, pl.ds(off, CH), :], (((1,), (1,)), ((), ())), preferred_element_type=jnp.float32)
            if masked:
                col = lax.broadcasted_iota(jnp.int32, (rows, CH), 1) + j * CH
                row = lax.broadcasted_iota(jnp.int32, (rows, CH), 0) % BLOCK
                ok = (col < n * BLOCK) & ((col >= BLOCK) | (col <= row))
                s = jnp.where(ok, s, NEG)
            return s

        def chunk(j, ms, masked, first):
            out = []
            off = pl.multiple_of(j * CH, CH)
            for r in range(NR):
                s = scores(r, j, masked)
                mx = jnp.max(s, axis=1, keepdims=True)
                if first:
                    mn = mx
                else:
                    mn = jnp.maximum(ms[r], mx)
                p = jnp.exp2(s * c2 - mn * c2).astype(jnp.bfloat16)
                pv = jnp.dot(p, vbuf[slot, pl.ds(off, CH), :], preferred_element_type=jnp.float32)
                if first:
                    acc[r] = pv
                else:
                    al = jnp.exp2((ms[r] - mn) * c2)
                    acc[r] = acc[r] * al + pv
                out.append(mn)
            return tuple(out)
        ms = chunk(jnp.int32(0), None, True, True)
        ms = lax.fori_loop(1, chunks - 1, lambda j, m: chunk(j, m, False, False), ms)
        @pl.when(chunks > 1)
        def _():
            chunk(chunks - 1, ms, True, False)
        for r in range(NR):
            o = acc[r, :, :D] / acc[r, :, D:]
            for g in range(RG):
                o_ref[h, pl.ds(row0, BLOCK), (r * RG + g) * D:(r * RG + g + 1) * D] = o[g * BLOCK:(g + 1) * BLOCK].astype(o_ref.dtype)
        return 0
    lax.fori_loop(0, steps, step_body, 0)

def attention(q, kv, vert, slash, ids, sinks, wins, pos, CH=512, RG=2, MODE=0):
    heads, toks, width = q.shape
    CB = CH // BLOCK
    slots = -(-33 // CB) * CB * BLOCK
    NR = width // D // RG
    sm = pl.BlockSpec(memory_space=pltpu.SMEM)
    return pl.pallas_call(
        functools.partial(attn_kernel, CH, RG, MODE),
        out_shape=jax.ShapeDtypeStruct(q.shape, jnp.bfloat16),
        in_specs=[sm] * 6 + [pl.BlockSpec(memory_space=pltpu.VMEM), pl.BlockSpec(memory_space=pl.ANY)],
        out_specs=pl.BlockSpec(memory_space=pltpu.VMEM),
        scratch_shapes=[
            pltpu.VMEM((2, slots, D), jnp.bfloat16),
            pltpu.VMEM((2, slots, 2 * D), jnp.bfloat16),
            pltpu.VMEM((8, 128), jnp.float32),
            pltpu.VMEM((NR, RG * BLOCK, 2 * D), jnp.float32),
            pltpu.SMEM((128,), jnp.int32),
            pltpu.SMEM((2,), jnp.int32),
            pltpu.SemaphoreType.DMA((2,)),
        ],
        compiler_params=pltpu.CompilerParams(vmem_limit_bytes=60 * 1024 * 1024),
    )(vert, slash, ids, sinks, wins, pos, q, kv)


def per_device(
    queries, keys, values, retrieval_ids, vertical_blocks, slash_offsets, sink_blocks, window_blocks
):
    position = jnp.stack([lax.axis_index("seq"), lax.axis_index("head")]).astype(jnp.int32)
    shard = jnp.stack([jnp.swapaxes(keys, 0, 1), jnp.swapaxes(values, 0, 1)], axis=1)
    gathered = lax.all_gather(shard, "seq", axis=0, tiled=False)
    out = attention(
        jnp.swapaxes(queries, 0, 1), gathered, vertical_blocks, slash_offsets,
        retrieval_ids, sink_blocks, window_blocks, position,
    )
    return jnp.swapaxes(out, 0, 1)


def solution(mesh):
    in_specs = (
        P("seq", "head", None),
        P("seq", "head", None),
        P("seq", "head", None),
        P(),
        P("seq", None, None),
        P("seq", None, None),
        P(),
        P(),
    )
    return jax.shard_map(
        per_device, mesh=mesh, in_specs=in_specs, out_specs=P("seq", "head", None), check_vma=False
    )
```

```python
import functools

import jax
import jax.numpy as jnp
from jax import lax
from jax.experimental import pallas as pl
from jax.experimental.pallas import tpu as pltpu
from jax.sharding import PartitionSpec as P

BLOCK=128; D=128; NEG=-1e30
LOG2E=1.4426950408889634

def attn_kernel(CH, RG, MODE, vert_ref, slash_ref, ids_ref, sink_ref, win_ref, pos_ref, q_ref, kv_ref, o_ref,
                kbuf, vbuf, sbuf, acc, stamp, cnt, sem):
    heads, toks, width = q_ref.shape
    G = width // D
    blocks_here = toks // BLOCK
    steps = heads * blocks_here
    first_block = pos_ref[0] * blocks_here
    first_head = pos_ref[1] * heads
    CB = CH // BLOCK
    rows = RG * BLOCK
    c2 = (D ** -0.5) * LOG2E

    def init(i, _):
        stamp[i] = -1
        return 0
    lax.fori_loop(0, 128, init, 0)
    vbuf[...] = jnp.zeros_like(vbuf)
    vbuf[:, :, D:] = jnp.ones((2, vbuf.shape[1], D), vbuf.dtype)
    kbuf[...] = jnp.zeros_like(kbuf)

    def copies(slot, h, c, n):
        src = kv_ref.at[c // 2, h]
        off = pl.multiple_of((c % 2) * BLOCK, BLOCK)
        dst = pl.multiple_of(n * BLOCK, BLOCK)
        return (pltpu.make_async_copy(src.at[0, pl.ds(off, BLOCK), :], kbuf.at[slot, pl.ds(dst, BLOCK), :], sem.at[slot]),
                pltpu.make_async_copy(src.at[1, pl.ds(off, BLOCK), :], vbuf.at[slot, pl.ds(dst, BLOCK), pl.ds(0, D)], sem.at[slot]))

    def fetch(step):
        slot = lax.rem(step, 2)
        h = step // blocks_here
        lb = lax.rem(step, blocks_here)
        head = first_head + h
        b = first_block + lb
        retr = (ids_ref[0] == head) | (ids_ref[1] == head) | (ids_ref[2] == head) | (ids_ref[3] == head)

        def add(c, ok, n):
            new = ok & (stamp[jnp.maximum(c, 0)] != step)
            @pl.when(new)
            def _():
                stamp[c] = step
                for cp in copies(slot, h, c, n):
                    cp.start()
            return n + new.astype(jnp.int32)

        n = add(b, True, jnp.int32(0))
        def retr_list(n):
            def one(j, n):
                n = add(vert_ref[lb, head, j], True, n)
                return add(b - slash_ref[lb, head, j], True, n)
            return lax.fori_loop(0, 16, one, n)
        def run_list(n):
            w = win_ref[head]; s = sink_ref[head]
            n = lax.fori_loop(0, jnp.minimum(s, b + 1), lambda c, n: add(c, True, n), n)
            return lax.fori_loop(1, jnp.minimum(w, b + 1), lambda d, n: add(b - d, True, n), n)
        n = lax.cond(retr, retr_list, run_list, n)
        cnt[slot] = n

    fetch(jnp.int32(0))

    def step_body(step, _):
        slot = lax.rem(step, 2)
        h = step // blocks_here
        lb = lax.rem(step, blocks_here)
        @pl.when(step + 1 < steps)
        def _():
            fetch(step + 1)
        n = cnt[slot]
        def wt(i, _):
            for cp in copies(slot, 0, 0, 0):
                cp.wait()
            return 0
        lax.fori_loop(0, n, wt, 0)
        row0 = pl.multiple_of(lb * BLOCK, BLOCK)
        chunks = (n + CB - 1) // CB
        def qrows(r):
            return jnp.concatenate([q_ref[h, pl.ds(row0, BLOCK), (r * RG + g) * D:(r * RG + g + 1) * D] for g in range(RG)], axis=0)
        NR = G // RG

        def scores(r, j, masked):
            off = pl.multiple_of(j * CH, CH)
            s = lax.dot_general(qrows(r), kbuf[slot, pl.ds(off, CH), :], (((1,), (1,)), ((), ())), preferred_element_type=jnp.float32)
            if masked:
                col = lax.broadcasted_iota(jnp.int32, (rows, CH), 1) + j * CH
                row = lax.broadcasted_iota(jnp.int32, (rows, CH), 0) % BLOCK
                ok = (col < n * BLOCK) & ((col >= BLOCK) | (col <= row))
                s = jnp.where(ok, s, NEG)
            return s

        def chunk(j, ms, masked, first):
            out = []
            off = pl.multiple_of(j * CH, CH)
            for r in range(NR):
                s = scores(r, j, masked)
                mx = jnp.max(s, axis=1, keepdims=True)
                if first:
                    mn = mx
                else:
                    mn = jnp.maximum(ms[r], mx)
                p = jnp.exp2(s * c2 - mn * c2).astype(jnp.bfloat16)
                pv = jnp.dot(p, vbuf[slot, pl.ds(off, CH), :], preferred_element_type=jnp.float32)
                if first:
                    acc[r] = pv
                else:
                    al = jnp.exp2((ms[r] - mn) * c2)
                    acc[r] = acc[r] * al + pv
                out.append(mn)
            return tuple(out)
        ms = chunk(jnp.int32(0), None, True, True)
        ms = lax.fori_loop(1, chunks - 1, lambda j, m: chunk(j, m, False, False), ms)
        @pl.when(chunks > 1)
        def _():
            chunk(chunks - 1, ms, True, False)
        for r in range(NR):
            o = acc[r, :, :D] / acc[r, :, D:]
            for g in range(RG):
                o_ref[h, pl.ds(row0, BLOCK), (r * RG + g) * D:(r * RG + g + 1) * D] = o[g * BLOCK:(g + 1) * BLOCK].astype(o_ref.dtype)
        return 0
    lax.fori_loop(0, steps, step_body, 0)

def attention(q, kv, vert, slash, ids, sinks, wins, pos, CH=512, RG=2, MODE=0):
    heads, toks, width = q.shape
    CB = CH // BLOCK
    slots = -(-33 // CB) * CB * BLOCK
    NR = width // D // RG
    sm = pl.BlockSpec(memory_space=pltpu.SMEM)
    return pl.pallas_call(
        functools.partial(attn_kernel, CH, RG, MODE),
        out_shape=jax.ShapeDtypeStruct(q.shape, jnp.bfloat16),
        in_specs=[sm] * 6 + [pl.BlockSpec(memory_space=pltpu.VMEM), pl.BlockSpec(memory_space=pl.ANY)],
        out_specs=pl.BlockSpec(memory_space=pltpu.VMEM),
        scratch_shapes=[
            pltpu.VMEM((2, slots, D), jnp.bfloat16),
            pltpu.VMEM((2, slots, 2 * D), jnp.bfloat16),
            pltpu.VMEM((8, 128), jnp.float32),
            pltpu.VMEM((NR, RG * BLOCK, 2 * D), jnp.float32),
            pltpu.SMEM((128,), jnp.int32),
            pltpu.SMEM((2,), jnp.int32),
            pltpu.SemaphoreType.DMA((2,)),
        ],
        compiler_params=pltpu.CompilerParams(vmem_limit_bytes=60 * 1024 * 1024),
    )(vert, slash, ids, sinks, wins, pos, q, kv)


MESH = pl.DeviceIdType.MESH


def gather_plan(ny, nz, a_rows, b_rows):
    half = {"A": a_rows // 2, "B": b_rows // 2}
    base = {"A": 0, "B": a_rows}
    size = {("A", 0): a_rows, ("B", 0): b_rows}

    def rows(part, sub):
        if sub == 0:
            return base[part], 2 * half[part]
        return base[part] + (sub - 1) * half[part], half[part]

    first = {"A": "z", "B": "y"}
    second = {"A": "y", "B": "z"}
    length = {"y": ny, "z": nz}
    free = {}
    heap = []
    seen_half = {}
    count = [0]
    order = []
    latency = 2.0
    rate = 46.5e3 / 256.0

    def move(off, axis, way):
        dy, dz = off
        if axis == "z":
            return dy, (dz - way) % nz
        return (dy - way) % ny, dz

    def send(part, sub, off, axis, way, now, sends):
        start, n = rows(part, sub)
        begin = max(now, free.get((axis, way), 0.0))
        end = begin + n / rate
        free[(axis, way)] = end
        count[0] += 1
        sends.append((part, sub, off, axis, way))
        heap.append((end + latency, count[0], part, sub, move(off, axis, way), axis, way))

    def complete(part, off, axis, now, sends):
        sends.append((part, 0, off, "c", 0))
        if axis == first[part]:
            for way in (1, -1):
                send(part, 0, off, second[part], way, now, sends)

    start = []
    for part in ("B", "A"):
        for way in (1, -1):
            send(part, 0, (0, 0), first[part], way, 0.0, start)
    for part in ("A", "B"):
        for way in (1, -1):
            send(part, 0, (0, 0), second[part], way, 0.0, start)
    for part in ("A", "B"):
        start.append((part, 0, (0, 0), "c", 0))
    finish = 0.0
    while heap:
        heap.sort()
        now, _, part, sub, off, axis, way = heap.pop(0)
        finish = max(finish, now)
        sends = []
        n = length[axis]
        d = off[1] if axis == "z" else off[0]
        dist = (-way * d) % n
        if sub == 0:
            if dist < n // 2 - 1:
                send(part, 0, off, axis, way, now, sends)
            else:
                send(part, 1 if way == 1 else 2, off, axis, way, now, sends)
            complete(part, off, axis, now, sends)
        else:
            key = (part, off, axis)
            seen_half[key] = seen_half.get(key, 0) + 1
            if seen_half[key] == 2:
                complete(part, off, axis, now, sends)
        order.append((part, sub, off, axis, sends))
    return start, order, rows, finish


def gather_kernel(ny, nz, a_rows, b_rows, shard_ref, out_ref, send_sem, recv_sem, local_sem):
    me = lax.axis_index("seq")
    y, z, core = me // (2 * nz), lax.rem(me // 2, nz), lax.rem(me, 2)
    start, order, rows, _ = gather_plan(ny, nz, a_rows, b_rows)

    def seq_of(dy, dz, c):
        return (lax.rem(y + dy, ny) * nz + lax.rem(z + dz, nz)) * 2 + c

    target = {
        ("y", 1): seq_of(1, 0, core), ("y", -1): seq_of(ny - 1, 0, core),
        ("z", 1): seq_of(0, 1, core), ("z", -1): seq_of(0, nz - 1, core),
        ("c", 0): seq_of(0, 0, 1 - core),
    }
    barrier = pltpu.get_barrier_semaphore()
    for t in target.values():
        pl.semaphore_signal(barrier, inc=1, device_id={"seq": t}, device_id_type=MESH)
    pl.semaphore_wait(barrier, len(target))

    own = pltpu.make_async_copy(shard_ref, out_ref.at[me], local_sem)
    own.start()

    def after(off, axis, way):
        dy, dz = off
        if axis == "z":
            return dy, (dz - way) % nz
        if axis == "y":
            return (dy - way) % ny, dz
        return off

    recv_id = {}
    send_id = [0]
    copies = {}

    def piece(part, sub, off, axis, way):
        to = after(off, axis, way)
        key = (part, sub, to, "c" if axis == "c" else "l")
        if key not in recv_id:
            recv_id[key] = len(recv_id)
        lo, n = rows(part, sub)
        place = out_ref.at[seq_of(off[0], off[1], core), pl.ds(lo, n), :]
        source = shard_ref.at[pl.ds(lo, n), :] if off == (0, 0) else place
        copy = pltpu.make_async_remote_copy(
            src_ref=source, dst_ref=place,
            send_sem=send_sem.at[send_id[0]], recv_sem=recv_sem.at[recv_id[key]],
            device_id={"seq": target[(axis, way)]}, device_id_type=MESH,
        )
        send_id[0] += 1
        copies[(part, sub, off, axis, way)] = copy
        return copy

    def arrival(part, sub, off, kind):
        key = (part, sub, off, kind)
        if key not in recv_id:
            recv_id[key] = len(recv_id)
        lo, n = rows(part, sub)
        c = core if kind == "l" else 1 - core
        place = out_ref.at[seq_of(off[0], off[1], c), pl.ds(lo, n), :]
        return pltpu.make_async_copy(place, place, recv_sem.at[recv_id[key]])

    for s in start:
        piece(*s).start()
    for part, sub, off, axis, sends in order:
        arrival(part, sub, off, "l").wait()
        for s in sends:
            piece(*s).start()
    for dy in range(ny):
        for dz in range(nz):
            for part in ("A", "B"):
                arrival(part, 0, (dy, dz), "c").wait()
    for copy in copies.values():
        copy.wait_send()
    own.wait()


def gather(shard, mesh_shape, a_rows, ny=4, nz=8):
    total = shard.shape[0]
    n_seq = mesh_shape["seq"]
    start, order, _, _ = gather_plan(ny, nz, a_rows, total - a_rows)
    n_send = len(start) + sum(len(o[-1]) for o in order)
    return pl.pallas_call(
        functools.partial(gather_kernel, ny, nz, a_rows, total - a_rows),
        out_shape=jax.ShapeDtypeStruct((n_seq,) + shard.shape, shard.dtype),
        in_specs=[pl.BlockSpec(memory_space=pl.ANY)],
        out_specs=pl.BlockSpec(memory_space=pl.ANY),
        scratch_shapes=[
            pltpu.SemaphoreType.DMA((n_send,)),
            pltpu.SemaphoreType.DMA((n_send,)),
            pltpu.SemaphoreType.DMA,
        ],
        compiler_params=pltpu.CompilerParams(collective_id=0, has_side_effects=True),
    )(shard)


def per_device(
    mesh_shape, queries, keys, values, retrieval_ids, vertical_blocks, slash_offsets, sink_blocks, window_blocks
):
    position = jnp.stack([lax.axis_index("seq"), lax.axis_index("head")]).astype(jnp.int32)
    tokens, heads, dim = keys.shape
    shard = jnp.stack([jnp.swapaxes(keys, 0, 1), jnp.swapaxes(values, 0, 1)], axis=1)
    gathered = gather(shard.reshape(-1, dim), mesh_shape, 640)
    out = attention(
        jnp.swapaxes(queries, 0, 1), gathered.reshape(-1, heads, 2, tokens, dim), vertical_blocks,
        slash_offsets, retrieval_ids, sink_blocks, window_blocks, position,
    )
    return jnp.swapaxes(out, 0, 1)


def solution(mesh):
    in_specs = (
        P("seq", "head", None),
        P("seq", "head", None),
        P("seq", "head", None),
        P(),
        P("seq", None, None),
        P("seq", None, None),
        P(),
        P(),
    )
    return jax.shard_map(
        functools.partial(per_device, mesh.shape), mesh=mesh, in_specs=in_specs,
        out_specs=P("seq", "head", None), check_vma=False,
    )
```

```python
import functools

import jax
import jax.numpy as jnp
from jax import lax
from jax.experimental import pallas as pl
from jax.experimental.pallas import tpu as pltpu
from jax.sharding import PartitionSpec as P

BLOCK = 128
D = 128
NEG = -1e30
LOG2E = 1.4426950408889634
LOW = 1e-25
HIGH = 1e25
CHUNK = 1024


def attn_kernel(vert_ref, slash_ref, ids_ref, sink_ref, win_ref, q_ref, o0_ref, flag_ref, kv0_ref, kv1_ref, o_ref,
                kbuf, vbuf, acc, result, stamp, cnt, sem):
    heads, toks, width = q_ref.shape
    G = width // D
    blocks_here = toks // BLOCK
    first_block = lax.axis_index("seq") * blocks_here
    first_head = lax.axis_index("head") * heads
    RG = 2
    rows = RG * BLOCK
    NR = G // RG
    CB = CHUNK // BLOCK
    c2 = (D ** -0.5) * LOG2E

    def clear(i, _):
        stamp[i] = -1
        return 0
    lax.fori_loop(0, 128, clear, 0)
    vbuf[...] = jnp.zeros_like(vbuf)
    kbuf[...] = jnp.zeros_like(kbuf)

    def copies(kv_ref, slot, c, n):
        dst = pl.multiple_of(n * BLOCK, BLOCK)
        return (
            pltpu.make_async_copy(kv_ref.at[c, pl.ds(0, BLOCK), :], kbuf.at[slot, pl.ds(dst, BLOCK), :], sem.at[slot]),
            pltpu.make_async_copy(kv_ref.at[c, pl.ds(BLOCK, BLOCK), :], vbuf.at[slot, pl.ds(dst, BLOCK), :], sem.at[slot]),
        )

    def fetch(kv_ref, h, lb, tag):
        slot = lb
        head = first_head + h
        b = first_block + lb
        retr = (ids_ref[0] == head) | (ids_ref[1] == head) | (ids_ref[2] == head) | (ids_ref[3] == head)

        def add(c, n):
            new = stamp[c] != tag

            @pl.when(new)
            def _():
                stamp[c] = tag
                for cp in copies(kv_ref, slot, c, n):
                    cp.start()
            return n + new.astype(jnp.int32)

        def retrieval(n):
            def one(j, n):
                return add(b - slash_ref[lb, head, j], add(vert_ref[lb, head, j], n))
            return lax.fori_loop(0, 16, one, n)

        def running(n):
            n = lax.fori_loop(0, jnp.minimum(sink_ref[head], b + 1), add, n)
            return lax.fori_loop(1, jnp.minimum(win_ref[head], b + 1), lambda d, n: add(b - d, n), n)
        cnt[slot] = lax.cond(retr, retrieval, running, add(b, jnp.int32(0)))

    def arrived(kv_ref, slot):
        def one(i, _):
            for cp in copies(kv_ref, slot, 0, 0):
                cp.wait()
            return 0
        lax.fori_loop(0, cnt[slot], one, 0)

    def query_rows(h, lb, r):
        row0 = pl.multiple_of(lb * BLOCK, BLOCK)
        return jnp.concatenate([q_ref[h, pl.ds(row0, BLOCK), (r * RG + g) * D:(r * RG + g + 1) * D] for g in range(RG)], axis=0)

    def attend(h, lb, off, length, bias, first):
        kt = kbuf[lb, pl.ds(off, length), :]
        v = vbuf[lb, pl.ds(off, length), :]
        va = jnp.concatenate([v, jnp.ones_like(v)], axis=1)
        for r in range(NR):
            s = lax.dot_general(query_rows(h, lb, r), kt, (((1,), (1,)), ((), ())), preferred_element_type=jnp.float32) * c2
            if bias is not None:
                s = jnp.concatenate([s[g * BLOCK:(g + 1) * BLOCK] + bias for g in range(RG)], axis=0)
            pv = jnp.dot(jnp.exp2(s).astype(jnp.bfloat16), va, preferred_element_type=jnp.float32)
            if first:
                acc[r] = pv
            else:
                acc[r] += pv

    def fast(h, lb):
        n = cnt[lb] - 1
        col = lax.broadcasted_iota(jnp.int32, (BLOCK, BLOCK), 1)
        row = lax.broadcasted_iota(jnp.int32, (BLOCK, BLOCK), 0)
        attend(h, lb, 0, BLOCK, jnp.where(col <= row, 0.0, NEG), True)
        whole = n // CB

        def chunk(j, _):
            attend(h, lb, pl.multiple_of(BLOCK + j * CHUNK, BLOCK), CHUNK, None, False)
            return 0
        lax.fori_loop(0, whole, chunk, 0)

        def small(j, _):
            off = pl.multiple_of(BLOCK + whole * CHUNK + j * 2 * BLOCK, BLOCK)
            left = (n - whole * CB - 2 * j) * BLOCK
            col = lax.broadcasted_iota(jnp.int32, (BLOCK, 2 * BLOCK), 1)
            attend(h, lb, off, 2 * BLOCK, jnp.where(col < left, 0.0, NEG), False)
            return 0
        lax.fori_loop(0, (n - whole * CB + 1) // 2, small, 0)

    def out_of_range():
        low = acc[0, :, D:]
        high = low
        for r in range(1, NR):
            t = acc[r, :, D:]
            low, high = jnp.minimum(low, t), jnp.maximum(high, t)
        return jnp.min(jnp.where((low > LOW) & (high < HIGH), 1.0, 0.0)) < 0.5

    def careful(h, lb):
        n = cnt[lb]
        length = 2 * BLOCK
        row0 = pl.multiple_of(lb * BLOCK, BLOCK)

        def group(r, _):
            qr = jnp.concatenate([
                q_ref[h, pl.ds(row0, BLOCK), pl.ds(pl.multiple_of((r * RG + g) * D, D), D)] for g in range(RG)], axis=0)

            def chunk(j, carry):
                m, a = carry
                off = pl.multiple_of(j * length, BLOCK)
                v = vbuf[lb, pl.ds(off, length), :]
                s = lax.dot_general(qr, kbuf[lb, pl.ds(off, length), :], (((1,), (1,)), ((), ())), preferred_element_type=jnp.float32)
                col = lax.broadcasted_iota(jnp.int32, (rows, length), 1) + off
                row = lax.broadcasted_iota(jnp.int32, (rows, length), 0) % BLOCK
                s = jnp.where((col < n * BLOCK) & ((col >= BLOCK) | (col <= row)), s, NEG)
                mn = jnp.maximum(m, jnp.max(s, axis=1, keepdims=True))
                p = jnp.exp2((s - mn) * c2).astype(jnp.bfloat16)
                pv = jnp.dot(p, jnp.concatenate([v, jnp.ones_like(v)], axis=1), preferred_element_type=jnp.float32)
                return mn, a * jnp.exp2((m - mn) * c2) + pv
            zero = (jnp.full((rows, 1), NEG, jnp.float32), jnp.zeros((rows, 2 * D), jnp.float32))
            acc[r] = lax.fori_loop(0, (n + 1) // 2, chunk, zero)[1]
            return 0
        lax.fori_loop(0, NR, group, 0)

    def store(h, lb):
        row0 = pl.multiple_of(lb * BLOCK, BLOCK)
        for r in range(NR):
            o = acc[r, :, :D] / acc[r, :, D:]
            for g in range(RG):
                result[h, pl.ds(row0, BLOCK), (r * RG + g) * D:(r * RG + g + 1) * D] = o[g * BLOCK:(g + 1) * BLOCK].astype(o_ref.dtype)

    for lb in range(blocks_here):
        fetch(kv1_ref, 1, jnp.int32(lb), lb)
    result[0] = o0_ref[...]

    def head1(lb, _):
        arrived(kv1_ref, lb)
        fast(1, lb)
        bad = out_of_range()

        @pl.when(bad)
        def _():
            careful(1, lb)
        store(1, lb)
        return 0
    lax.fori_loop(0, blocks_here, head1, 0)

    def head0(lb, _):
        bad = jnp.min(flag_ref[lb]) < 0.5

        @pl.when(bad)
        def _():
            fetch(kv0_ref, 0, lb, blocks_here + lb)
            arrived(kv0_ref, lb)
            careful(0, lb)
            store(0, lb)
        return 0
    lax.fori_loop(0, blocks_here, head0, 0)
    for h in range(heads):
        o_ref[:, h, :] = result[h]


def attention(q, o0, flag, kv0, kv1, vert, slash, ids, sinks, wins):
    heads, toks, width = q.shape
    sm = pl.BlockSpec(memory_space=pltpu.SMEM)
    vm = pl.BlockSpec(memory_space=pltpu.VMEM)
    hbm = pl.BlockSpec(memory_space=pl.ANY)
    slots = 34 * BLOCK
    return pl.pallas_call(
        attn_kernel,
        out_shape=jax.ShapeDtypeStruct((toks, heads, width), jnp.bfloat16),
        in_specs=[sm] * 5 + [vm] * 3 + [hbm] * 2,
        out_specs=vm,
        scratch_shapes=[
            pltpu.VMEM((2, slots, D), jnp.bfloat16),
            pltpu.VMEM((2, slots, D), jnp.bfloat16),
            pltpu.VMEM((width // D // 2, 2 * BLOCK, 2 * D), jnp.float32),
            pltpu.VMEM((heads, toks, width), jnp.bfloat16),
            pltpu.SMEM((128,), jnp.int32),
            pltpu.SMEM((2,), jnp.int32),
            pltpu.SemaphoreType.DMA((2,)),
        ],
        compiler_params=pltpu.CompilerParams(vmem_limit_bytes=60 * 1024 * 1024),
    )(vert, slash, ids, sinks, wins, q, o0, flag, kv0, kv1)


MESH = pl.DeviceIdType.MESH
LISTED = 33
NY = 4
NZ = 8


def gather_plan(ny, nz, layers, a_rows, b_rows, starts):
    half = {"A": a_rows // 2, "B": b_rows // 2}
    base = {"A": 0, "B": a_rows}
    first = {"A": "z", "B": "y"}
    second = {"A": "y", "B": "z"}
    length = {"y": ny, "z": nz}
    latency, rate, near = 2.0, 46.5e3 / 512.0, 300e3 / 512.0

    def rows(part, sub):
        if sub == 0:
            return base[part], 2 * half[part]
        return base[part] + (sub - 1) * half[part], half[part]

    free, halves = {}, {}
    heap = []
    count = [0]
    order = []

    def push(time, what):
        count[0] += 1
        heap.append((time, count[0], what))

    def send(layer, part, sub, off, axis, way, now, sends):
        n = rows(part, sub)[1]
        begin = max(now, free.get((axis, way), 0.0))
        end = begin + n / (near if axis == "c" else rate)
        free[(axis, way)] = end
        sends.append((layer, part, sub, off, axis, way))
        dy, dz = off
        if axis == "z":
            dz = (dz - way) % nz
        if axis == "y":
            dy = (dy - way) % ny
        push(end + (1.0 if axis == "c" else latency), (layer, part, sub, (dy, dz), axis, way))

    def complete(layer, part, off, axis, now, sends):
        send(layer, part, 0, off, "c", 0, now, sends)
        if axis == first[part]:
            for way in (1, -1):
                send(layer, part, 0, off, second[part], way, now, sends)

    for layer in range(layers):
        push(starts[layer], (layer, None))
    while heap:
        heap.sort(key=lambda e: e[:2])
        now, _, what = heap.pop(0)
        sends = []
        if what[1] is None:
            layer = what[0]
            for part in ("B", "A"):
                for way in (1, -1):
                    send(layer, part, 0, (0, 0), first[part], way, now, sends)
            for part in ("A", "B"):
                for way in (1, -1):
                    send(layer, part, 0, (0, 0), second[part], way, now, sends)
                send(layer, part, 0, (0, 0), "c", 0, now, sends)
            order.append((now, what, sends))
            continue
        layer, part, sub, off, axis, way = what
        if axis != "c":
            n = length[axis]
            dist = (-way * (off[1] if axis == "z" else off[0])) % n
            if sub == 0:
                if dist < n // 2 - 1:
                    send(layer, part, 0, off, axis, way, now, sends)
                else:
                    send(layer, part, 1 if way == 1 else 2, off, axis, way, now, sends)
                complete(layer, part, off, axis, now, sends)
            else:
                key = (layer, part, off, axis)
                halves[key] = halves.get(key, 0) + 1
                if halves[key] == 2:
                    complete(layer, part, off, axis, now, sends)
        order.append((now, what, sends))
    return order, rows


def gather_kernel(a_rows, start1, unit_us, vert_ref, slash_ref, ids_ref, sink_ref, win_ref, q_ref, k_ref, v_ref,
                  kv0_out, kv1_out, qt_out, o_ref, flag_ref,
                  kv0, shard, qt, acc, cand, usable, send_sem, recv_sem, local_sem):
    ny, nz = NY, NZ
    me = lax.axis_index("seq")
    head_slot = lax.axis_index("head")
    toks, heads, width = q_ref.shape
    dim = k_ref.shape[2]
    G = width // dim
    blocks_here = toks // BLOCK
    y, z, core = me // (2 * nz), lax.rem(me // 2, nz), lax.rem(me, 2)
    order, rows = gather_plan(ny, nz, 2, a_rows, 2 * BLOCK - a_rows, (0.0, start1))
    c2 = (dim ** -0.5) * LOG2E

    for h in range(heads):
        for lb in range(blocks_here):
            shard[h, lb, :BLOCK, :] = k_ref[lb * BLOCK:(lb + 1) * BLOCK, h, :]
            shard[h, lb, BLOCK:, :] = v_ref[lb * BLOCK:(lb + 1) * BLOCK, h, :]

    def seq_of(dy, dz, c):
        return (lax.rem(y + dy, ny) * nz + lax.rem(z + dz, nz)) * 2 + c

    target = {
        ("y", 1): seq_of(1, 0, core), ("y", -1): seq_of(ny - 1, 0, core),
        ("z", 1): seq_of(0, 1, core), ("z", -1): seq_of(0, nz - 1, core),
        ("c", 0): seq_of(0, 0, 1 - core),
    }
    barrier = pltpu.get_barrier_semaphore()
    for t in target.values():
        pl.semaphore_signal(barrier, inc=1, device_id={"seq": t}, device_id_type=MESH)
    pl.semaphore_wait(barrier, len(target))

    held = (kv0, kv1_out)

    def blocks_of(seq):
        return pl.ds(seq * blocks_here, blocks_here)
    own = [pltpu.make_async_copy(shard.at[layer], held[layer].at[blocks_of(me)], local_sem.at[layer]) for layer in range(2)]
    for copy in own:
        copy.start()
    recv_id = {}
    copies = []

    def number(key):
        return recv_id.setdefault(key, len(recv_id))

    def piece(layer, part, sub, off, axis, way):
        dy, dz = off
        to = (dy, (dz - way) % nz) if axis == "z" else ((dy - way) % ny, dz) if axis == "y" else off
        lo, n = rows(part, sub)
        place = held[layer].at[blocks_of(seq_of(dy, dz, core)), pl.ds(lo, n), :]
        source = shard.at[layer, :, pl.ds(lo, n), :] if off == (0, 0) else place
        copy = pltpu.make_async_remote_copy(
            src_ref=source, dst_ref=place,
            send_sem=send_sem.at[len(copies)],
            recv_sem=recv_sem.at[number((layer, part, sub, to, axis == "c"))],
            device_id={"seq": target[(axis, way)]}, device_id_type=MESH,
        )
        copies.append(copy)
        return copy

    def arrive(what):
        layer, part, sub, off, axis, _ = what
        lo, n = rows(part, sub)
        place = held[layer].at[blocks_of(seq_of(off[0], off[1], 1 - core if axis == "c" else core)), pl.ds(lo, n), :]
        pltpu.make_async_copy(place, place, recv_sem.at[number((layer, part, sub, off, axis == "c"))]).wait()

    def handle(event):
        _, what, sends = event
        if what[1] is not None:
            arrive(what)
        for s in sends:
            piece(*s).start()

    head0 = head_slot * heads

    def one_if(condition):
        return condition.astype(jnp.int32)
    hits = one_if(ids_ref[0] == head0) + one_if(ids_ref[1] == head0) + one_if(ids_ref[2] == head0) + one_if(ids_ref[3] == head0)
    retr = one_if(hits > 0)

    def list_blocks(lb):
        b = me * blocks_here + lb
        sinks, wins = sink_ref[head0], win_ref[head0]
        at = lb * 64
        cand[at] = b
        usable[at] = 1
        for j in range(1, LISTED):
            listed = vert_ref[lb, head0, j - 1] if j <= 16 else b - slash_ref[lb, head0, j - 17]
            if j <= 2:
                read = j - 1
                ok = one_if(j - 1 < sinks) * one_if(j - 1 <= b)
            elif j <= 6:
                read = b - (j - 2)
                ok = one_if(j - 2 < wins) * one_if(j - 2 <= b)
            else:
                read, ok = -1 - j, 0
            ok = retr + (1 - retr) * ok
            cand[at + j] = ok * (retr * listed + (1 - retr) * read) - (1 - ok) * (1 + j)

        def mark(j, _):
            mine = cand[at + j]
            same = 0
            for k in range(LISTED):
                same = same + one_if(k < j) * one_if(cand[at + k] == mine)
            usable[at + j] = one_if(mine >= 0) * one_if(same == 0)
            return 0
        lax.fori_loop(1, LISTED, mark, 0)

    def query_rows(lb, r):
        return jnp.concatenate([qt[0, lb * BLOCK:(lb + 1) * BLOCK, (2 * r + g) * dim:(2 * r + g + 1) * dim] for g in range(2)], axis=0)

    def attend(lb, kt, va, bias):
        for r in range(G // 2):
            s = lax.dot_general(query_rows(lb, r), kt, (((1,), (1,)), ((), ())), preferred_element_type=jnp.float32) * c2
            if bias is not None:
                s = jnp.concatenate([s[:BLOCK] + bias, s[BLOCK:] + bias], axis=0)
            pv = jnp.dot(jnp.exp2(s).astype(jnp.bfloat16), va, preferred_element_type=jnp.float32)
            if bias is not None:
                acc[r] = pv
            else:
                acc[r] += pv

    def diagonal(lb):
        kt = shard[0, lb, :BLOCK, :]
        v = shard[0, lb, BLOCK:, :]
        col = lax.broadcasted_iota(jnp.int32, (BLOCK, BLOCK), 1)
        row = lax.broadcasted_iota(jnp.int32, (BLOCK, BLOCK), 0)
        attend(lb, kt, jnp.concatenate([v, jnp.ones_like(v)], axis=1), jnp.where(col <= row, 0.0, NEG))

    def listed_blocks(lb, j0, count):
        ks, vs = [], []
        for j in range(count):
            c = jnp.minimum(jnp.maximum(cand[lb * 64 + j0 + j], 0), kv0.shape[0] - 1)
            weight = usable[lb * 64 + j0 + j].astype(jnp.float32)
            weights = jnp.full((BLOCK, dim), weight, jnp.float32).astype(jnp.bfloat16)
            ks.append(kv0[c, :BLOCK, :])
            vs.append(jnp.concatenate([kv0[c, BLOCK:, :] * weights, weights], axis=1))
        attend(lb, jnp.concatenate(ks, axis=0), jnp.concatenate(vs, axis=0), None)

    def finish(lb):
        low = acc[0, :, dim:]
        high = low
        for r in range(G // 2):
            t = acc[r, :, dim:]
            o = acc[r, :, :dim] / t
            low, high = jnp.minimum(low, t), jnp.maximum(high, t)
            for g in range(2):
                o_ref[lb * BLOCK:(lb + 1) * BLOCK, (2 * r + g) * dim:(2 * r + g + 1) * dim] = o[g * BLOCK:(g + 1) * BLOCK].astype(o_ref.dtype)
        flag_ref[lb] = jnp.where((low > LOW) & (high < HIGH), 1.0, 0.0)

    span = 8
    units = []
    for lb in range(blocks_here):
        units.append(functools.partial(diagonal, lb))
        for j0 in range(1, LISTED, span):
            units.append(functools.partial(listed_blocks, lb, j0, span))
        units.append(functools.partial(finish, lb))
    spare = [functools.partial(list_blocks, lb) for lb in range(blocks_here)]

    def split_queries(i):
        for h in range(heads):
            qt[h, i * 64:(i + 1) * 64, :] = q_ref[i * 64:(i + 1) * 64, h, :]
    spare += [functools.partial(split_queries, i) for i in range(toks // 64)]

    last0 = max(i for i, e in enumerate(order) if e[1][0] == 0)
    tail = []
    own[0].wait()
    for i, event in enumerate(order[:last0 + 1]):
        handle(event)
        if i % 8 == 2 and spare:
            spare.pop(0)()
    for work in spare:
        work()
    keep = pltpu.make_async_copy(kv0, kv0_out, local_sem.at[2])
    keep.start()
    keep_q = pltpu.make_async_copy(qt, qt_out, local_sem.at[3])
    keep_q.start()
    rest = order[last0 + 1:]
    clock = order[last0][0]
    for work in units:
        while rest and rest[0][0] <= clock:
            handle(rest.pop(0))
        work()
        if work.func is listed_blocks:
            clock += unit_us
    for event in rest:
        handle(event)
    for copy in copies:
        copy.wait_send()
    own[1].wait()
    keep.wait()
    keep_q.wait()


def gather(queries, keys, values, vert, slash, ids, sinks, wins, n_seq, a_rows=160, start1=23.0, unit_us=1.7):
    toks, heads, width = queries.shape
    dim = keys.shape[2]
    order, _ = gather_plan(NY, NZ, 2, a_rows, 2 * BLOCK - a_rows, (0.0, start1))
    n_send = sum(len(e[2]) for e in order)
    sm = pl.BlockSpec(memory_space=pltpu.SMEM)
    vm = pl.BlockSpec(memory_space=pltpu.VMEM)
    hbm = pl.BlockSpec(memory_space=pl.ANY)
    bf = jnp.bfloat16
    return pl.pallas_call(
        functools.partial(gather_kernel, a_rows, start1, unit_us),
        out_shape=(
            jax.ShapeDtypeStruct((n_seq * toks // BLOCK, 2 * BLOCK, dim), bf),
            jax.ShapeDtypeStruct((n_seq * toks // BLOCK, 2 * BLOCK, dim), bf),
            jax.ShapeDtypeStruct((heads, toks, width), bf),
            jax.ShapeDtypeStruct((toks, width), bf),
            jax.ShapeDtypeStruct((toks // BLOCK, 2 * BLOCK, dim), jnp.float32),
        ),
        in_specs=[sm] * 5 + [vm] * 3,
        out_specs=(hbm, hbm, hbm, vm, vm),
        scratch_shapes=[
            pltpu.VMEM((n_seq * toks // BLOCK, 2 * BLOCK, dim), bf),
            pltpu.VMEM((heads, toks // BLOCK, 2 * BLOCK, dim), bf),
            pltpu.VMEM((heads, toks, width), bf),
            pltpu.VMEM((width // dim // 2, 2 * BLOCK, 2 * dim), jnp.float32),
            pltpu.SMEM((toks // BLOCK * 64,), jnp.int32),
            pltpu.SMEM((toks // BLOCK * 64,), jnp.int32),
            pltpu.SemaphoreType.DMA((n_send,)),
            pltpu.SemaphoreType.DMA((n_send,)),
            pltpu.SemaphoreType.DMA((4,)),
        ],
        compiler_params=pltpu.CompilerParams(
            collective_id=0, has_side_effects=True, vmem_limit_bytes=60 * 1024 * 1024,
        ),
    )(vert, slash, ids, sinks, wins, queries, keys, values)


def per_device(
    n_seq, queries, keys, values, retrieval_ids, vertical_blocks, slash_offsets, sink_blocks, window_blocks
):
    lists = (vertical_blocks, slash_offsets, retrieval_ids, sink_blocks, window_blocks)
    kv0, kv1, q, o0, flag = gather(queries, keys, values, *lists, n_seq)
    return attention(q, o0, flag, kv0, kv1, *lists)


def solution(mesh):
    in_specs = (
        P("seq", "head", None),
        P("seq", "head", None),
        P("seq", "head", None),
        P(),
        P("seq", None, None),
        P("seq", None, None),
        P(),
        P(),
    )
    return jax.shard_map(
        functools.partial(per_device, mesh.shape["seq"]), mesh=mesh, in_specs=in_specs,
        out_specs=P("seq", "head", None), check_vma=False,
    )
```

```python
import functools

import jax
import jax.numpy as jnp
from jax import lax
from jax.experimental import pallas as pl
from jax.experimental.pallas import tpu as pltpu
from jax.sharding import PartitionSpec as P

BLOCK = 128
D = 128
NEG = -1e30
LOG2E = 1.4426950408889634
LOW = 1e-25
HIGH = 1e25
CHUNK = 1024


def attn_kernel(vert_ref, slash_ref, ids_ref, sink_ref, win_ref, q_ref, o0_ref, flag_ref, kv0_ref, kv1_ref, o_ref,
                kbuf, vbuf, acc, result, stamp, cnt, sem):
    heads, toks, width = q_ref.shape
    G = width // D
    blocks_here = toks // BLOCK
    first_block = lax.axis_index("seq") * blocks_here
    first_head = lax.axis_index("head") * heads
    RG = 2
    rows = RG * BLOCK
    NR = G // RG
    CB = CHUNK // BLOCK
    c2 = (D ** -0.5) * LOG2E

    def clear(i, _):
        stamp[i] = -1
        return 0
    lax.fori_loop(0, 128, clear, 0)

    def copies(kv_ref, slot, c, n):
        dst = pl.multiple_of(n * BLOCK, BLOCK)
        return (
            pltpu.make_async_copy(kv_ref.at[c, pl.ds(0, BLOCK), :], kbuf.at[slot, pl.ds(dst, BLOCK), :], sem.at[slot]),
            pltpu.make_async_copy(kv_ref.at[c, pl.ds(BLOCK, BLOCK), :], vbuf.at[slot, pl.ds(dst, BLOCK), :], sem.at[slot]),
        )

    def fetch(kv_ref, h, lb, tag):
        slot = lb
        head = first_head + h
        b = first_block + lb
        retr = (ids_ref[0] == head) | (ids_ref[1] == head) | (ids_ref[2] == head) | (ids_ref[3] == head)

        def add(c, n):
            new = stamp[c] != tag

            @pl.when(new)
            def _():
                stamp[c] = tag
                for cp in copies(kv_ref, slot, c, n):
                    cp.start()
            return n + new.astype(jnp.int32)

        def retrieval(n):
            def one(j, n):
                return add(b - slash_ref[lb, head, j], add(vert_ref[lb, head, j], n))
            return lax.fori_loop(0, 16, one, n)

        def running(n):
            n = lax.fori_loop(0, jnp.minimum(sink_ref[head], b + 1), add, n)
            return lax.fori_loop(1, jnp.minimum(win_ref[head], b + 1), lambda d, n: add(b - d, n), n)
        cnt[slot] = lax.cond(retr, retrieval, running, add(b, jnp.int32(0)))

    def arrived(kv_ref, slot):
        def one(i, _):
            for cp in copies(kv_ref, slot, 0, 0):
                cp.wait()
            return 0
        lax.fori_loop(0, cnt[slot], one, 0)
        pad = pl.ds(pl.multiple_of(cnt[slot] * BLOCK, BLOCK), BLOCK)
        kbuf[slot, pad, :] = jnp.zeros((BLOCK, D), kbuf.dtype)
        vbuf[slot, pad, :] = jnp.zeros((BLOCK, D), vbuf.dtype)

    def query_rows(h, lb, r):
        row0 = pl.multiple_of(lb * BLOCK, BLOCK)
        return jnp.concatenate([q_ref[h, pl.ds(row0, BLOCK), (r * RG + g) * D:(r * RG + g + 1) * D] for g in range(RG)], axis=0)

    def attend(h, lb, off, length, bias, first):
        kt = kbuf[lb, pl.ds(off, length), :]
        v = vbuf[lb, pl.ds(off, length), :]
        va = jnp.concatenate([v, jnp.ones_like(v)], axis=1)
        for r in range(NR):
            s = lax.dot_general(query_rows(h, lb, r), kt, (((1,), (1,)), ((), ())), preferred_element_type=jnp.float32) * c2
            if bias is not None:
                s = jnp.concatenate([s[g * BLOCK:(g + 1) * BLOCK] + bias for g in range(RG)], axis=0)
            pv = jnp.dot(jnp.exp2(s).astype(jnp.bfloat16), va, preferred_element_type=jnp.float32)
            if first:
                acc[r] = pv
            else:
                acc[r] += pv

    def fast(h, lb):
        n = cnt[lb] - 1
        col = lax.broadcasted_iota(jnp.int32, (BLOCK, BLOCK), 1)
        row = lax.broadcasted_iota(jnp.int32, (BLOCK, BLOCK), 0)
        attend(h, lb, 0, BLOCK, jnp.where(col <= row, 0.0, NEG), True)
        whole = n // CB

        def chunk(j, _):
            attend(h, lb, pl.multiple_of(BLOCK + j * CHUNK, BLOCK), CHUNK, None, False)
            return 0
        lax.fori_loop(0, whole, chunk, 0)

        def small(j, _):
            off = pl.multiple_of(BLOCK + whole * CHUNK + j * 2 * BLOCK, BLOCK)
            left = (n - whole * CB - 2 * j) * BLOCK
            col = lax.broadcasted_iota(jnp.int32, (BLOCK, 2 * BLOCK), 1)
            attend(h, lb, off, 2 * BLOCK, jnp.where(col < left, 0.0, NEG), False)
            return 0
        lax.fori_loop(0, (n - whole * CB + 1) // 2, small, 0)

    def out_of_range():
        low = acc[0, :, D:]
        high = low
        for r in range(1, NR):
            t = acc[r, :, D:]
            low, high = jnp.minimum(low, t), jnp.maximum(high, t)
        return jnp.min(jnp.where((low > LOW) & (high < HIGH), 1.0, 0.0)) < 0.5

    def careful(h, lb):
        n = cnt[lb]
        length = 2 * BLOCK
        row0 = pl.multiple_of(lb * BLOCK, BLOCK)

        def group(r, _):
            qr = jnp.concatenate([
                q_ref[h, pl.ds(row0, BLOCK), pl.ds(pl.multiple_of((r * RG + g) * D, D), D)] for g in range(RG)], axis=0)

            def chunk(j, carry):
                m, a = carry
                off = pl.multiple_of(j * length, BLOCK)
                v = vbuf[lb, pl.ds(off, length), :]
                s = lax.dot_general(qr, kbuf[lb, pl.ds(off, length), :], (((1,), (1,)), ((), ())), preferred_element_type=jnp.float32)
                col = lax.broadcasted_iota(jnp.int32, (rows, length), 1) + off
                row = lax.broadcasted_iota(jnp.int32, (rows, length), 0) % BLOCK
                s = jnp.where((col < n * BLOCK) & ((col >= BLOCK) | (col <= row)), s, NEG)
                mn = jnp.maximum(m, jnp.max(s, axis=1, keepdims=True))
                p = jnp.exp2((s - mn) * c2).astype(jnp.bfloat16)
                pv = jnp.dot(p, jnp.concatenate([v, jnp.ones_like(v)], axis=1), preferred_element_type=jnp.float32)
                return mn, a * jnp.exp2((m - mn) * c2) + pv
            zero = (jnp.full((rows, 1), NEG, jnp.float32), jnp.zeros((rows, 2 * D), jnp.float32))
            acc[r] = lax.fori_loop(0, (n + 1) // 2, chunk, zero)[1]
            return 0
        lax.fori_loop(0, NR, group, 0)

    def store(h, lb):
        row0 = pl.multiple_of(lb * BLOCK, BLOCK)
        for r in range(NR):
            o = acc[r, :, :D] / acc[r, :, D:]
            for g in range(RG):
                result[h, pl.ds(row0, BLOCK), (r * RG + g) * D:(r * RG + g + 1) * D] = o[g * BLOCK:(g + 1) * BLOCK].astype(o_ref.dtype)

    for lb in range(blocks_here):
        fetch(kv1_ref, 1, jnp.int32(lb), lb)
    result[0] = o0_ref[...]

    def head1(lb, _):
        arrived(kv1_ref, lb)
        fast(1, lb)
        bad = out_of_range()

        @pl.when(bad)
        def _():
            careful(1, lb)
        store(1, lb)
        return 0
    lax.fori_loop(0, blocks_here, head1, 0)

    def head0(lb, _):
        bad = jnp.min(flag_ref[lb]) < 0.5

        @pl.when(bad)
        def _():
            fetch(kv0_ref, 0, lb, blocks_here + lb)
            arrived(kv0_ref, lb)
            careful(0, lb)
            store(0, lb)
        return 0
    lax.fori_loop(0, blocks_here, head0, 0)
    for h in range(heads):
        o_ref[:, h, :] = result[h]


def attention(q, o0, flag, kv0, kv1, vert, slash, ids, sinks, wins):
    heads, toks, width = q.shape
    sm = pl.BlockSpec(memory_space=pltpu.SMEM)
    vm = pl.BlockSpec(memory_space=pltpu.VMEM)
    hbm = pl.BlockSpec(memory_space=pl.ANY)
    slots = 34 * BLOCK
    return pl.pallas_call(
        attn_kernel,
        out_shape=jax.ShapeDtypeStruct((toks, heads, width), jnp.bfloat16),
        in_specs=[sm] * 5 + [vm] * 3 + [hbm] * 2,
        out_specs=vm,
        scratch_shapes=[
            pltpu.VMEM((2, slots, D), jnp.bfloat16),
            pltpu.VMEM((2, slots, D), jnp.bfloat16),
            pltpu.VMEM((width // D // 2, 2 * BLOCK, 2 * D), jnp.float32),
            pltpu.VMEM((heads, toks, width), jnp.bfloat16),
            pltpu.SMEM((128,), jnp.int32),
            pltpu.SMEM((2,), jnp.int32),
            pltpu.SemaphoreType.DMA((2,)),
        ],
        compiler_params=pltpu.CompilerParams(vmem_limit_bytes=60 * 1024 * 1024),
    )(vert, slash, ids, sinks, wins, q, o0, flag, kv0, kv1)


MESH = pl.DeviceIdType.MESH
LISTED = 33
NY = 4
NZ = 8


def gather_plan(ny, nz, layers, a_rows, b_rows, starts):
    half = {"A": a_rows // 2, "B": b_rows // 2}
    base = {"A": 0, "B": a_rows}
    first = {"A": "z", "B": "y"}
    second = {"A": "y", "B": "z"}
    length = {"y": ny, "z": nz}
    latency, rate, near = 2.0, 46.5e3 / 512.0, 300e3 / 512.0

    def rows(part, sub):
        if part == "W":
            return 0, a_rows + b_rows
        if sub == 0:
            return base[part], 2 * half[part]
        return base[part] + (sub - 1) * half[part], half[part]

    free, halves, whole = {}, {}, {}
    heap = []
    count = [0]
    order = []

    def push(time, what):
        count[0] += 1
        heap.append((time, count[0], what))

    def send(layer, part, sub, off, axis, way, now, sends):
        n = rows(part, sub)[1]
        begin = max(now, free.get((axis, way), 0.0))
        end = begin + n / (near if axis == "c" else rate)
        free[(axis, way)] = end
        sends.append((layer, part, sub, off, axis, way))
        dy, dz = off
        if axis == "z":
            dz = (dz - way) % nz
        if axis == "y":
            dy = (dy - way) % ny
        push(end + (1.0 if axis == "c" else latency), (layer, part, sub, (dy, dz), axis, way))

    def complete(layer, part, off, axis, now, sends):
        whole[(layer, off)] = whole.get((layer, off), 0) + 1
        if whole[(layer, off)] == 2:
            send(layer, "W", 0, off, "c", 0, now, sends)
        if axis == first[part]:
            for way in (1, -1):
                send(layer, part, 0, off, second[part], way, now, sends)

    for layer in range(layers):
        push(starts[layer], (layer, None))
    while heap:
        heap.sort(key=lambda e: e[:2])
        now, _, what = heap.pop(0)
        sends = []
        if what[1] is None:
            layer = what[0]
            for part in ("B", "A"):
                for way in (1, -1):
                    send(layer, part, 0, (0, 0), first[part], way, now, sends)
            for part in ("A", "B"):
                for way in (1, -1):
                    send(layer, part, 0, (0, 0), second[part], way, now, sends)
            send(layer, "W", 0, (0, 0), "c", 0, now, sends)
            order.append((now, what, sends))
            continue
        layer, part, sub, off, axis, way = what
        if axis != "c":
            n = length[axis]
            dist = (-way * (off[1] if axis == "z" else off[0])) % n
            if sub == 0:
                if dist < n // 2 - 1:
                    send(layer, part, 0, off, axis, way, now, sends)
                else:
                    send(layer, part, 1 if way == 1 else 2, off, axis, way, now, sends)
                complete(layer, part, off, axis, now, sends)
            else:
                key = (layer, part, off, axis)
                halves[key] = halves.get(key, 0) + 1
                if halves[key] == 2:
                    complete(layer, part, off, axis, now, sends)
        order.append((now, what, sends))
    return order, rows


def gather_kernel(a_rows, start1, unit_us, vert_ref, slash_ref, ids_ref, sink_ref, win_ref, q_ref, k_ref, v_ref,
                  kv0_out, kv1_out, qt_out, o_ref, flag_ref,
                  kv0, shard, qt, acc, cand, usable, send_sem, recv_sem, local_sem):
    ny, nz = NY, NZ
    me = lax.axis_index("seq")
    head_slot = lax.axis_index("head")
    toks, heads, width = q_ref.shape
    dim = k_ref.shape[2]
    G = width // dim
    blocks_here = toks // BLOCK
    y, z, core = me // (2 * nz), lax.rem(me // 2, nz), lax.rem(me, 2)
    order, rows = gather_plan(ny, nz, 2, a_rows, 2 * BLOCK - a_rows, (0.0, start1))
    c2 = (dim ** -0.5) * LOG2E

    for h in range(heads):
        for lb in range(blocks_here):
            shard[h, lb, :BLOCK, :] = k_ref[lb * BLOCK:(lb + 1) * BLOCK, h, :]
            shard[h, lb, BLOCK:, :] = v_ref[lb * BLOCK:(lb + 1) * BLOCK, h, :]

    def seq_of(dy, dz, c):
        return (lax.rem(y + dy, ny) * nz + lax.rem(z + dz, nz)) * 2 + c

    target = {
        ("y", 1): seq_of(1, 0, core), ("y", -1): seq_of(ny - 1, 0, core),
        ("z", 1): seq_of(0, 1, core), ("z", -1): seq_of(0, nz - 1, core),
        ("c", 0): seq_of(0, 0, 1 - core),
    }
    barrier = pltpu.get_barrier_semaphore()
    for t in target.values():
        pl.semaphore_signal(barrier, inc=1, device_id={"seq": t}, device_id_type=MESH)
    pl.semaphore_wait(barrier, len(target))

    held = (kv0, kv1_out)

    def blocks_of(seq):
        return pl.ds(seq * blocks_here, blocks_here)
    own = [pltpu.make_async_copy(shard.at[layer], held[layer].at[blocks_of(me)], local_sem.at[layer]) for layer in range(2)]
    for copy in own:
        copy.start()
    recv_id = {}
    copies = []

    def number(key):
        return recv_id.setdefault(key, len(recv_id))

    def piece(layer, part, sub, off, axis, way):
        dy, dz = off
        to = (dy, (dz - way) % nz) if axis == "z" else ((dy - way) % ny, dz) if axis == "y" else off
        lo, n = rows(part, sub)
        place = held[layer].at[blocks_of(seq_of(dy, dz, core)), pl.ds(lo, n), :]
        source = shard.at[layer, :, pl.ds(lo, n), :] if off == (0, 0) else place
        copy = pltpu.make_async_remote_copy(
            src_ref=source, dst_ref=place,
            send_sem=send_sem.at[len(copies)],
            recv_sem=recv_sem.at[number((layer, part, sub, to, axis == "c"))],
            device_id={"seq": target[(axis, way)]}, device_id_type=MESH,
        )
        copies.append(copy)
        return copy

    def arrive(what):
        layer, part, sub, off, axis, _ = what
        lo, n = rows(part, sub)
        place = held[layer].at[blocks_of(seq_of(off[0], off[1], 1 - core if axis == "c" else core)), pl.ds(lo, n), :]
        pltpu.make_async_copy(place, place, recv_sem.at[number((layer, part, sub, off, axis == "c"))]).wait()

    def handle(event):
        _, what, sends = event
        if what[1] is not None:
            arrive(what)
        for s in sends:
            piece(*s).start()

    head0 = head_slot * heads

    def one_if(condition):
        return condition.astype(jnp.int32)
    hits = one_if(ids_ref[0] == head0) + one_if(ids_ref[1] == head0) + one_if(ids_ref[2] == head0) + one_if(ids_ref[3] == head0)
    retr = one_if(hits > 0)

    def list_blocks(lb):
        b = me * blocks_here + lb
        sinks, wins = sink_ref[head0], win_ref[head0]
        at = lb * 64
        cand[at] = b
        usable[at] = 1
        for j in range(1, LISTED):
            listed = vert_ref[lb, head0, j - 1] if j <= 16 else b - slash_ref[lb, head0, j - 17]
            if j <= 2:
                read = j - 1
                ok = one_if(j - 1 < sinks) * one_if(j - 1 <= b)
            elif j <= 6:
                read = b - (j - 2)
                ok = one_if(j - 2 < wins) * one_if(j - 2 <= b)
            else:
                read, ok = -1 - j, 0
            ok = retr + (1 - retr) * ok
            cand[at + j] = ok * (retr * listed + (1 - retr) * read) - (1 - ok) * (1 + j)

        def mark(j, _):
            mine = cand[at + j]
            same = 0
            for k in range(LISTED):
                same = same + one_if(k < j) * one_if(cand[at + k] == mine)
            usable[at + j] = one_if(mine >= 0) * one_if(same == 0)
            return 0
        lax.fori_loop(1, LISTED, mark, 0)

    def query_rows(lb, r):
        return jnp.concatenate([qt[0, lb * BLOCK:(lb + 1) * BLOCK, (2 * r + g) * dim:(2 * r + g + 1) * dim] for g in range(2)], axis=0)

    def attend(lb, kt, va, bias):
        for r in range(G // 2):
            s = lax.dot_general(query_rows(lb, r), kt, (((1,), (1,)), ((), ())), preferred_element_type=jnp.float32) * c2
            if bias is not None:
                s = jnp.concatenate([s[:BLOCK] + bias, s[BLOCK:] + bias], axis=0)
            pv = jnp.dot(jnp.exp2(s).astype(jnp.bfloat16), va, preferred_element_type=jnp.float32)
            if bias is not None:
                acc[r] = pv
            else:
                acc[r] += pv

    def diagonal(lb):
        kt = shard[0, lb, :BLOCK, :]
        v = shard[0, lb, BLOCK:, :]
        col = lax.broadcasted_iota(jnp.int32, (BLOCK, BLOCK), 1)
        row = lax.broadcasted_iota(jnp.int32, (BLOCK, BLOCK), 0)
        attend(lb, kt, jnp.concatenate([v, jnp.ones_like(v)], axis=1), jnp.where(col <= row, 0.0, NEG))

    def listed_blocks(lb, j0, count):
        ks, vs = [], []
        for j in range(count):
            c = jnp.minimum(jnp.maximum(cand[lb * 64 + j0 + j], 0), kv0.shape[0] - 1)
            weight = usable[lb * 64 + j0 + j].astype(jnp.float32)
            weights = jnp.full((BLOCK, dim), weight, jnp.float32).astype(jnp.bfloat16)
            ks.append(kv0[c, :BLOCK, :])
            vs.append(jnp.concatenate([kv0[c, BLOCK:, :] * weights, weights], axis=1))
        attend(lb, jnp.concatenate(ks, axis=0), jnp.concatenate(vs, axis=0), None)

    def finish(lb):
        low = acc[0, :, dim:]
        high = low
        for r in range(G // 2):
            t = acc[r, :, dim:]
            o = acc[r, :, :dim] / t
            low, high = jnp.minimum(low, t), jnp.maximum(high, t)
            for g in range(2):
                o_ref[lb * BLOCK:(lb + 1) * BLOCK, (2 * r + g) * dim:(2 * r + g + 1) * dim] = o[g * BLOCK:(g + 1) * BLOCK].astype(o_ref.dtype)
        flag_ref[lb] = jnp.where((low > LOW) & (high < HIGH), 1.0, 0.0)

    span = 8
    units = []
    for lb in range(blocks_here):
        units.append(functools.partial(diagonal, lb))
        for j0 in range(1, LISTED, span):
            units.append(functools.partial(listed_blocks, lb, j0, span))
        units.append(functools.partial(finish, lb))
    spare = [functools.partial(list_blocks, lb) for lb in range(blocks_here)]

    def split_queries(i):
        for h in range(heads):
            qt[h, i * 64:(i + 1) * 64, :] = q_ref[i * 64:(i + 1) * 64, h, :]
    spare += [functools.partial(split_queries, i) for i in range(toks // 64)]

    last0 = max(i for i, e in enumerate(order) if e[1][0] == 0)
    tail = []
    own[0].wait()
    for i, event in enumerate(order[:last0 + 1]):
        handle(event)
        if i % 8 == 2 and spare:
            spare.pop(0)()
    for work in spare:
        work()
    keep = pltpu.make_async_copy(kv0, kv0_out, local_sem.at[2])
    keep.start()
    keep_q = pltpu.make_async_copy(qt, qt_out, local_sem.at[3])
    keep_q.start()
    rest = order[last0 + 1:]
    clock = order[last0][0]
    for work in units:
        while rest and rest[0][0] <= clock:
            handle(rest.pop(0))
        work()
        if work.func is listed_blocks:
            clock += unit_us
    for event in rest:
        handle(event)
    for copy in copies:
        copy.wait_send()
    own[1].wait()
    keep.wait()
    keep_q.wait()


def gather(queries, keys, values, vert, slash, ids, sinks, wins, n_seq, a_rows=160, start1=16.0, unit_us=1.7):
    toks, heads, width = queries.shape
    dim = keys.shape[2]
    order, _ = gather_plan(NY, NZ, 2, a_rows, 2 * BLOCK - a_rows, (0.0, start1))
    n_send = sum(len(e[2]) for e in order)
    sm = pl.BlockSpec(memory_space=pltpu.SMEM)
    vm = pl.BlockSpec(memory_space=pltpu.VMEM)
    hbm = pl.BlockSpec(memory_space=pl.ANY)
    bf = jnp.bfloat16
    return pl.pallas_call(
        functools.partial(gather_kernel, a_rows, start1, unit_us),
        out_shape=(
            jax.ShapeDtypeStruct((n_seq * toks // BLOCK, 2 * BLOCK, dim), bf),
            jax.ShapeDtypeStruct((n_seq * toks // BLOCK, 2 * BLOCK, dim), bf),
            jax.ShapeDtypeStruct((heads, toks, width), bf),
            jax.ShapeDtypeStruct((toks, width), bf),
            jax.ShapeDtypeStruct((toks // BLOCK, 2 * BLOCK, dim), jnp.float32),
        ),
        in_specs=[sm] * 5 + [vm] * 3,
        out_specs=(hbm, hbm, hbm, vm, vm),
        scratch_shapes=[
            pltpu.VMEM((n_seq * toks // BLOCK, 2 * BLOCK, dim), bf),
            pltpu.VMEM((heads, toks // BLOCK, 2 * BLOCK, dim), bf),
            pltpu.VMEM((heads, toks, width), bf),
            pltpu.VMEM((width // dim // 2, 2 * BLOCK, 2 * dim), jnp.float32),
            pltpu.SMEM((toks // BLOCK * 64,), jnp.int32),
            pltpu.SMEM((toks // BLOCK * 64,), jnp.int32),
            pltpu.SemaphoreType.DMA((n_send,)),
            pltpu.SemaphoreType.DMA((n_send,)),
            pltpu.SemaphoreType.DMA((4,)),
        ],
        compiler_params=pltpu.CompilerParams(
            collective_id=0, has_side_effects=True, vmem_limit_bytes=60 * 1024 * 1024,
        ),
    )(vert, slash, ids, sinks, wins, queries, keys, values)


def per_device(
    n_seq, queries, keys, values, retrieval_ids, vertical_blocks, slash_offsets, sink_blocks, window_blocks
):
    lists = (vertical_blocks, slash_offsets, retrieval_ids, sink_blocks, window_blocks)
    kv0, kv1, q, o0, flag = gather(queries, keys, values, *lists, n_seq)
    return attention(q, o0, flag, kv0, kv1, *lists)


def solution(mesh):
    in_specs = (
        P("seq", "head", None),
        P("seq", "head", None),
        P("seq", "head", None),
        P(),
        P("seq", None, None),
        P("seq", None, None),
        P(),
        P(),
    )
    return jax.shard_map(
        functools.partial(per_device, mesh.shape["seq"]), mesh=mesh, in_specs=in_specs,
        out_specs=P("seq", "head", None), check_vma=False,
    )
```

```python
import functools

import jax
import jax.numpy as jnp
from jax import lax
from jax.experimental import pallas as pl
from jax.experimental.pallas import tpu as pltpu
from jax.sharding import PartitionSpec as P

BLOCK = 128
D = 128
NEG = -1e30
LOG2E = 1.4426950408889634
LOW = 1e-25
HIGH = 1e25
CHUNK = 1024


def attn_kernel(vert_ref, slash_ref, ids_ref, sink_ref, win_ref, q_ref, o0_ref, flag_ref, kv0_ref, kv1_ref, o_ref,
                kbuf, vbuf, acc, result, stamp, cnt, sem):
    heads, toks, width = q_ref.shape
    G = width // D
    blocks_here = toks // BLOCK
    first_block = lax.axis_index("seq") * blocks_here
    first_head = lax.axis_index("head") * heads
    RG = 2
    rows = RG * BLOCK
    NR = G // RG
    CB = CHUNK // BLOCK
    c2 = (D ** -0.5) * LOG2E

    def clear(i, _):
        stamp[i] = -1
        return 0
    lax.fori_loop(0, 128, clear, 0)

    def copies(kv_ref, slot, c, n):
        dst = pl.multiple_of(n * BLOCK, BLOCK)
        return (
            pltpu.make_async_copy(kv_ref.at[c, pl.ds(0, BLOCK), :], kbuf.at[slot, pl.ds(dst, BLOCK), :], sem.at[slot]),
            pltpu.make_async_copy(kv_ref.at[c, pl.ds(BLOCK, BLOCK), :], vbuf.at[slot, pl.ds(dst, BLOCK), :], sem.at[slot]),
        )

    def fetch(kv_ref, h, lb, tag):
        slot = lb
        head = first_head + h
        b = first_block + lb
        retr = (ids_ref[0] == head) | (ids_ref[1] == head) | (ids_ref[2] == head) | (ids_ref[3] == head)

        def add(c, n):
            new = stamp[c] != tag

            @pl.when(new)
            def _():
                stamp[c] = tag
                for cp in copies(kv_ref, slot, c, n):
                    cp.start()
            return n + new.astype(jnp.int32)

        def retrieval(n):
            def one(j, n):
                return add(b - slash_ref[lb, head, j], add(vert_ref[lb, head, j], n))
            return lax.fori_loop(0, 16, one, n)

        def running(n):
            n = lax.fori_loop(0, jnp.minimum(sink_ref[head], b + 1), add, n)
            return lax.fori_loop(1, jnp.minimum(win_ref[head], b + 1), lambda d, n: add(b - d, n), n)
        cnt[slot] = lax.cond(retr, retrieval, running, add(b, jnp.int32(0)))

    def arrived(kv_ref, slot):
        def one(i, _):
            for cp in copies(kv_ref, slot, 0, 0):
                cp.wait()
            return 0
        lax.fori_loop(0, cnt[slot], one, 0)
        pad = pl.ds(pl.multiple_of(cnt[slot] * BLOCK, BLOCK), BLOCK)
        kbuf[slot, pad, :] = jnp.zeros((BLOCK, D), kbuf.dtype)
        vbuf[slot, pad, :] = jnp.zeros((BLOCK, D), vbuf.dtype)

    def query_rows(h, lb, r):
        row0 = pl.multiple_of(lb * BLOCK, BLOCK)
        return jnp.concatenate([q_ref[h, pl.ds(row0, BLOCK), (r * RG + g) * D:(r * RG + g + 1) * D] for g in range(RG)], axis=0)

    def attend(h, lb, off, length, bias, first):
        kt = kbuf[lb, pl.ds(off, length), :]
        v = vbuf[lb, pl.ds(off, length), :]
        va = jnp.concatenate([v, jnp.ones_like(v)], axis=1)
        for r in range(NR):
            s = lax.dot_general(query_rows(h, lb, r), kt, (((1,), (1,)), ((), ())), preferred_element_type=jnp.float32) * c2
            if bias is not None:
                s = jnp.concatenate([s[g * BLOCK:(g + 1) * BLOCK] + bias for g in range(RG)], axis=0)
            pv = jnp.dot(jnp.exp2(s).astype(jnp.bfloat16), va, preferred_element_type=jnp.float32)
            if first:
                acc[r] = pv
            else:
                acc[r] += pv

    def fast(h, lb):
        n = cnt[lb] - 1
        col = lax.broadcasted_iota(jnp.int32, (BLOCK, BLOCK), 1)
        row = lax.broadcasted_iota(jnp.int32, (BLOCK, BLOCK), 0)
        attend(h, lb, 0, BLOCK, jnp.where(col <= row, 0.0, NEG), True)
        whole = n // CB

        def chunk(j, _):
            attend(h, lb, pl.multiple_of(BLOCK + j * CHUNK, BLOCK), CHUNK, None, False)
            return 0
        lax.fori_loop(0, whole, chunk, 0)

        def small(j, _):
            off = pl.multiple_of(BLOCK + whole * CHUNK + j * 2 * BLOCK, BLOCK)
            left = (n - whole * CB - 2 * j) * BLOCK
            col = lax.broadcasted_iota(jnp.int32, (BLOCK, 2 * BLOCK), 1)
            attend(h, lb, off, 2 * BLOCK, jnp.where(col < left, 0.0, NEG), False)
            return 0
        lax.fori_loop(0, (n - whole * CB + 1) // 2, small, 0)

    def out_of_range():
        low = acc[0, :, D:]
        high = low
        for r in range(1, NR):
            t = acc[r, :, D:]
            low, high = jnp.minimum(low, t), jnp.maximum(high, t)
        return jnp.min(jnp.where((low > LOW) & (high < HIGH), 1.0, 0.0)) < 0.5

    def careful(h, lb):
        n = cnt[lb]
        length = 2 * BLOCK
        row0 = pl.multiple_of(lb * BLOCK, BLOCK)

        def group(r, _):
            qr = jnp.concatenate([
                q_ref[h, pl.ds(row0, BLOCK), pl.ds(pl.multiple_of((r * RG + g) * D, D), D)] for g in range(RG)], axis=0)

            def chunk(j, carry):
                m, a = carry
                off = pl.multiple_of(j * length, BLOCK)
                v = vbuf[lb, pl.ds(off, length), :]
                s = lax.dot_general(qr, kbuf[lb, pl.ds(off, length), :], (((1,), (1,)), ((), ())), preferred_element_type=jnp.float32)
                col = lax.broadcasted_iota(jnp.int32, (rows, length), 1) + off
                row = lax.broadcasted_iota(jnp.int32, (rows, length), 0) % BLOCK
                s = jnp.where((col < n * BLOCK) & ((col >= BLOCK) | (col <= row)), s, NEG)
                mn = jnp.maximum(m, jnp.max(s, axis=1, keepdims=True))
                p = jnp.exp2((s - mn) * c2).astype(jnp.bfloat16)
                pv = jnp.dot(p, jnp.concatenate([v, jnp.ones_like(v)], axis=1), preferred_element_type=jnp.float32)
                return mn, a * jnp.exp2((m - mn) * c2) + pv
            zero = (jnp.full((rows, 1), NEG, jnp.float32), jnp.zeros((rows, 2 * D), jnp.float32))
            acc[r] = lax.fori_loop(0, (n + 1) // 2, chunk, zero)[1]
            return 0
        lax.fori_loop(0, NR, group, 0)

    def store(h, lb):
        row0 = pl.multiple_of(lb * BLOCK, BLOCK)
        for r in range(NR):
            o = acc[r, :, :D] / acc[r, :, D:]
            for g in range(RG):
                result[h, pl.ds(row0, BLOCK), (r * RG + g) * D:(r * RG + g + 1) * D] = o[g * BLOCK:(g + 1) * BLOCK].astype(o_ref.dtype)

    for lb in range(blocks_here):
        fetch(kv1_ref, 1, jnp.int32(lb), lb)
    result[0] = o0_ref[...]

    def head1(lb, _):
        arrived(kv1_ref, lb)
        fast(1, lb)
        bad = out_of_range()

        @pl.when(bad)
        def _():
            careful(1, lb)
        store(1, lb)
        return 0
    lax.fori_loop(0, blocks_here, head1, 0)

    def head0(lb, _):
        bad = jnp.min(flag_ref[lb]) < 0.5

        @pl.when(bad)
        def _():
            fetch(kv0_ref, 0, lb, blocks_here + lb)
            arrived(kv0_ref, lb)
            careful(0, lb)
            store(0, lb)
        return 0
    lax.fori_loop(0, blocks_here, head0, 0)
    for h in range(heads):
        o_ref[:, h, :] = result[h]


def attention(q, o0, flag, kv0, kv1, vert, slash, ids, sinks, wins):
    heads, toks, width = q.shape
    sm = pl.BlockSpec(memory_space=pltpu.SMEM)
    vm = pl.BlockSpec(memory_space=pltpu.VMEM)
    hbm = pl.BlockSpec(memory_space=pl.ANY)
    slots = 34 * BLOCK
    return pl.pallas_call(
        attn_kernel,
        out_shape=jax.ShapeDtypeStruct((toks, heads, width), jnp.bfloat16),
        in_specs=[sm] * 5 + [vm] * 3 + [hbm] * 2,
        out_specs=vm,
        scratch_shapes=[
            pltpu.VMEM((2, slots, D), jnp.bfloat16),
            pltpu.VMEM((2, slots, D), jnp.bfloat16),
            pltpu.VMEM((width // D // 2, 2 * BLOCK, 2 * D), jnp.float32),
            pltpu.VMEM((heads, toks, width), jnp.bfloat16),
            pltpu.SMEM((128,), jnp.int32),
            pltpu.SMEM((2,), jnp.int32),
            pltpu.SemaphoreType.DMA((2,)),
        ],
        compiler_params=pltpu.CompilerParams(vmem_limit_bytes=60 * 1024 * 1024),
    )(vert, slash, ids, sinks, wins, q, o0, flag, kv0, kv1)


MESH = pl.DeviceIdType.MESH
LISTED = 33
NY = 4
NZ = 8


def gather_plan(ny, nz, layers, a_rows, b_rows, starts):
    half = {"A": a_rows // 2, "B": b_rows // 2}
    base = {"A": 0, "B": a_rows}
    first = {"A": "z", "B": "y"}
    second = {"A": "y", "B": "z"}
    length = {"y": ny, "z": nz}
    latency, rate, near = 2.0, 46.5e3 / 512.0, 300e3 / 512.0

    def rows(part, sub):
        if part == "W":
            return 0, a_rows + b_rows
        if sub == 0:
            return base[part], 2 * half[part]
        return base[part] + (sub - 1) * half[part], half[part]

    free, halves, whole = {}, {}, {}
    heap = []
    count = [0]
    order = []

    def push(time, what):
        count[0] += 1
        heap.append((time, count[0], what))

    def send(layer, part, sub, off, axis, way, now, sends):
        n = rows(part, sub)[1]
        begin = max(now, free.get((axis, way), 0.0))
        share = near if axis == "c" else 2.0 * rate * (length[axis] // 2 - (way < 0)) / (length[axis] - 1)
        end = begin + n / share
        free[(axis, way)] = end
        sends.append((layer, part, sub, off, axis, way))
        dy, dz = off
        if axis == "z":
            dz = (dz - way) % nz
        if axis == "y":
            dy = (dy - way) % ny
        push(end + (1.0 if axis == "c" else latency), (layer, part, sub, (dy, dz), axis, way))

    def complete(layer, part, off, axis, now, sends):
        whole[(layer, off)] = whole.get((layer, off), 0) + 1
        if whole[(layer, off)] == 2:
            send(layer, "W", 0, off, "c", 0, now, sends)
        if axis == first[part]:
            for way in (1, -1):
                send(layer, part, 0, off, second[part], way, now, sends)

    for layer in range(layers):
        push(starts[layer], (layer, None))
    while heap:
        heap.sort(key=lambda e: e[:2])
        now, _, what = heap.pop(0)
        sends = []
        if what[1] is None:
            layer = what[0]
            for part in ("B", "A"):
                for way in (1, -1):
                    send(layer, part, 0, (0, 0), first[part], way, now, sends)
            for part in ("A", "B"):
                for way in (1, -1):
                    send(layer, part, 0, (0, 0), second[part], way, now, sends)
            send(layer, "W", 0, (0, 0), "c", 0, now, sends)
            order.append((now, what, sends))
            continue
        layer, part, sub, off, axis, way = what
        if axis != "c":
            n = length[axis]
            dist = (-way * (off[1] if axis == "z" else off[0])) % n
            if dist < n // 2 - (way < 0):
                send(layer, part, 0, off, axis, way, now, sends)
            complete(layer, part, off, axis, now, sends)
        order.append((now, what, sends))
    return order, rows


def gather_kernel(a_rows, start1, unit_us, vert_ref, slash_ref, ids_ref, sink_ref, win_ref, q_ref, k_ref, v_ref,
                  kv0_out, kv1_out, qt_out, o_ref, flag_ref,
                  kv0, shard, qt, acc, cand, usable, send_sem, whole_sem, recv_sem, local_sem):
    ny, nz = NY, NZ
    me = lax.axis_index("seq")
    head_slot = lax.axis_index("head")
    toks, heads, width = q_ref.shape
    dim = k_ref.shape[2]
    G = width // dim
    blocks_here = toks // BLOCK
    y, z, core = me // (2 * nz), lax.rem(me // 2, nz), lax.rem(me, 2)
    turn = 1 - 2 * core
    order, rows = gather_plan(ny, nz, 2, a_rows, 2 * BLOCK - a_rows, (0.0, start1))
    c2 = (dim ** -0.5) * LOG2E

    for h in range(heads):
        for lb in range(blocks_here):
            shard[h, lb, :BLOCK, :] = k_ref[lb * BLOCK:(lb + 1) * BLOCK, h, :]
            shard[h, lb, BLOCK:, :] = v_ref[lb * BLOCK:(lb + 1) * BLOCK, h, :]

    def seq_of(dy, dz, c):
        return (lax.rem(y + turn * dy + ny, ny) * nz + lax.rem(z + turn * dz + nz, nz)) * 2 + c

    target = {
        ("y", 1): seq_of(1, 0, core), ("y", -1): seq_of(ny - 1, 0, core),
        ("z", 1): seq_of(0, 1, core), ("z", -1): seq_of(0, nz - 1, core),
        ("c", 0): seq_of(0, 0, 1 - core),
    }
    barrier = pltpu.get_barrier_semaphore()
    for t in target.values():
        pl.semaphore_signal(barrier, inc=1, device_id={"seq": t}, device_id_type=MESH)
    pl.semaphore_wait(barrier, len(target))

    held = (kv0, kv1_out)

    def blocks_of(seq):
        return pl.ds(seq * blocks_here, blocks_here)
    own = [pltpu.make_async_copy(shard.at[layer], held[layer].at[blocks_of(me)], local_sem.at[layer]) for layer in range(2)]
    for copy in own:
        copy.start()
    recv_id = {}

    def number(key):
        return recv_id.setdefault(key, len(recv_id))

    def piece(layer, part, sub, off, axis, way):
        dy, dz = off
        to = (dy, (dz - way) % nz) if axis == "z" else ((dy - way) % ny, dz) if axis == "y" else off
        lo, n = rows(part, sub)
        place = held[layer].at[blocks_of(seq_of(dy, dz, core)), pl.ds(lo, n), :]
        source = shard.at[layer, :, pl.ds(lo, n), :] if off == (0, 0) else place
        copy = pltpu.make_async_remote_copy(
            src_ref=source, dst_ref=place,
            send_sem=send_sem.at[layer],
            recv_sem=whole_sem.at[layer] if axis == "c" else recv_sem.at[number((layer, part, sub, to))],
            device_id={"seq": target[(axis, way)]}, device_id_type=MESH,
        )
        return copy

    def arrive(what):
        layer, part, sub, off, _, _ = what
        lo, n = rows(part, sub)
        place = held[layer].at[blocks_of(seq_of(off[0], off[1], core)), pl.ds(lo, n), :]
        pltpu.make_async_copy(place, place, recv_sem.at[number((layer, part, sub, off))]).wait()

    def await_bytes(layer, blocks, sem):
        place = held[layer].at[pl.ds(0, blocks)]
        pltpu.make_async_copy(place, place, sem.at[layer]).wait()

    def handle(event):
        _, what, sends = event
        if what[1] not in (None, "W"):
            arrive(what)
        for s in sends:
            piece(*s).start()

    head0 = head_slot * heads

    def one_if(condition):
        return condition.astype(jnp.int32)
    hits = one_if(ids_ref[0] == head0) + one_if(ids_ref[1] == head0) + one_if(ids_ref[2] == head0) + one_if(ids_ref[3] == head0)
    retr = one_if(hits > 0)

    def list_blocks(lb):
        b = me * blocks_here + lb
        sinks, wins = sink_ref[head0], win_ref[head0]
        at = lb * 64
        cand[at] = b
        usable[at] = 1
        for j in range(1, LISTED):
            listed = vert_ref[lb, head0, j - 1] if j <= 16 else b - slash_ref[lb, head0, j - 17]
            if j <= 2:
                read = j - 1
                ok = one_if(j - 1 < sinks) * one_if(j - 1 <= b)
            elif j <= 6:
                read = b - (j - 2)
                ok = one_if(j - 2 < wins) * one_if(j - 2 <= b)
            else:
                read, ok = -1 - j, 0
            ok = retr + (1 - retr) * ok
            cand[at + j] = ok * (retr * listed + (1 - retr) * read) - (1 - ok) * (1 + j)

        def mark(j, _):
            mine = cand[at + j]
            same = 0
            for k in range(LISTED):
                same = same + one_if(k < j) * one_if(cand[at + k] == mine)
            usable[at + j] = one_if(mine >= 0) * one_if(same == 0)
            return 0
        lax.fori_loop(1, LISTED, mark, 0)

    def query_rows(lb, r):
        return jnp.concatenate([qt[0, lb * BLOCK:(lb + 1) * BLOCK, (2 * r + g) * dim:(2 * r + g + 1) * dim] for g in range(2)], axis=0)

    def attend(lb, kt, va, bias):
        for r in range(G // 2):
            s = lax.dot_general(query_rows(lb, r), kt, (((1,), (1,)), ((), ())), preferred_element_type=jnp.float32) * c2
            if bias is not None:
                s = jnp.concatenate([s[:BLOCK] + bias, s[BLOCK:] + bias], axis=0)
            pv = jnp.dot(jnp.exp2(s).astype(jnp.bfloat16), va, preferred_element_type=jnp.float32)
            if bias is not None:
                acc[r] = pv
            else:
                acc[r] += pv

    def diagonal(lb):
        kt = shard[0, lb, :BLOCK, :]
        v = shard[0, lb, BLOCK:, :]
        col = lax.broadcasted_iota(jnp.int32, (BLOCK, BLOCK), 1)
        row = lax.broadcasted_iota(jnp.int32, (BLOCK, BLOCK), 0)
        attend(lb, kt, jnp.concatenate([v, jnp.ones_like(v)], axis=1), jnp.where(col <= row, 0.0, NEG))

    def listed_blocks(lb, j0, count):
        ks, vs = [], []
        for j in range(count):
            c = jnp.minimum(jnp.maximum(cand[lb * 64 + j0 + j], 0), kv0.shape[0] - 1)
            weight = usable[lb * 64 + j0 + j].astype(jnp.float32)
            weights = jnp.full((BLOCK, dim), weight, jnp.float32).astype(jnp.bfloat16)
            ks.append(kv0[c, :BLOCK, :])
            vs.append(jnp.concatenate([kv0[c, BLOCK:, :] * weights, weights], axis=1))
        attend(lb, jnp.concatenate(ks, axis=0), jnp.concatenate(vs, axis=0), None)

    def finish(lb):
        low = acc[0, :, dim:]
        high = low
        for r in range(G // 2):
            t = acc[r, :, dim:]
            o = acc[r, :, :dim] / t
            low, high = jnp.minimum(low, t), jnp.maximum(high, t)
            for g in range(2):
                o_ref[lb * BLOCK:(lb + 1) * BLOCK, (2 * r + g) * dim:(2 * r + g + 1) * dim] = o[g * BLOCK:(g + 1) * BLOCK].astype(o_ref.dtype)
        flag_ref[lb] = jnp.where((low > LOW) & (high < HIGH), 1.0, 0.0)

    span = 8
    units = []
    for lb in range(blocks_here):
        units.append(functools.partial(diagonal, lb))
        for j0 in range(1, LISTED, span):
            units.append(functools.partial(listed_blocks, lb, j0, span))
        units.append(functools.partial(finish, lb))
    spare = [functools.partial(list_blocks, lb) for lb in range(blocks_here)]

    def split_queries(i):
        for h in range(heads):
            qt[h, i * 64:(i + 1) * 64, :] = q_ref[i * 64:(i + 1) * 64, h, :]
    spare += [functools.partial(split_queries, i) for i in range(toks // 64)]

    last0 = max(i for i, e in enumerate(order) if e[1][0] == 0)
    tail = []
    own[0].wait()
    for i, event in enumerate(order[:last0 + 1]):
        handle(event)
        if i % 8 == 2 and spare:
            spare.pop(0)()
    for work in spare:
        work()
    total = kv0.shape[0]
    await_bytes(0, total // 2, whole_sem)
    keep = pltpu.make_async_copy(kv0, kv0_out, local_sem.at[2])
    keep.start()
    keep_q = pltpu.make_async_copy(qt, qt_out, local_sem.at[3])
    keep_q.start()
    rest = order[last0 + 1:]
    clock = order[last0][0]
    for work in units:
        while rest and rest[0][0] <= clock:
            handle(rest.pop(0))
        work()
        if work.func is listed_blocks:
            clock += unit_us
    for event in rest:
        handle(event)
    await_bytes(1, total // 2, whole_sem)
    for layer in range(2):
        await_bytes(layer, total - blocks_here, send_sem)
    own[1].wait()
    keep.wait()
    keep_q.wait()


def gather(queries, keys, values, vert, slash, ids, sinks, wins, n_seq, a_rows=160, start1=14.0, unit_us=1.7):
    toks, heads, width = queries.shape
    dim = keys.shape[2]
    order, _ = gather_plan(NY, NZ, 2, a_rows, 2 * BLOCK - a_rows, (0.0, start1))
    arrivals = sum(e[1][1] not in (None, "W") for e in order)
    sm = pl.BlockSpec(memory_space=pltpu.SMEM)
    vm = pl.BlockSpec(memory_space=pltpu.VMEM)
    hbm = pl.BlockSpec(memory_space=pl.ANY)
    bf = jnp.bfloat16
    return pl.pallas_call(
        functools.partial(gather_kernel, a_rows, start1, unit_us),
        out_shape=(
            jax.ShapeDtypeStruct((n_seq * toks // BLOCK, 2 * BLOCK, dim), bf),
            jax.ShapeDtypeStruct((n_seq * toks // BLOCK, 2 * BLOCK, dim), bf),
            jax.ShapeDtypeStruct((heads, toks, width), bf),
            jax.ShapeDtypeStruct((toks, width), bf),
            jax.ShapeDtypeStruct((toks // BLOCK, 2 * BLOCK, dim), jnp.float32),
        ),
        in_specs=[sm] * 5 + [vm] * 3,
        out_specs=(hbm, hbm, hbm, vm, vm),
        scratch_shapes=[
            pltpu.VMEM((n_seq * toks // BLOCK, 2 * BLOCK, dim), bf),
            pltpu.VMEM((heads, toks // BLOCK, 2 * BLOCK, dim), bf),
            pltpu.VMEM((heads, toks, width), bf),
            pltpu.VMEM((width // dim // 2, 2 * BLOCK, 2 * dim), jnp.float32),
            pltpu.SMEM((toks // BLOCK * 64,), jnp.int32),
            pltpu.SMEM((toks // BLOCK * 64,), jnp.int32),
            pltpu.SemaphoreType.DMA((2,)),
            pltpu.SemaphoreType.DMA((2,)),
            pltpu.SemaphoreType.DMA((arrivals,)),
            pltpu.SemaphoreType.DMA((4,)),
        ],
        compiler_params=pltpu.CompilerParams(
            collective_id=0, has_side_effects=True, vmem_limit_bytes=60 * 1024 * 1024,
        ),
    )(vert, slash, ids, sinks, wins, queries, keys, values)


def per_device(
    n_seq, queries, keys, values, retrieval_ids, vertical_blocks, slash_offsets, sink_blocks, window_blocks
):
    lists = (vertical_blocks, slash_offsets, retrieval_ids, sink_blocks, window_blocks)
    kv0, kv1, q, o0, flag = gather(queries, keys, values, *lists, n_seq)
    return attention(q, o0, flag, kv0, kv1, *lists)


def solution(mesh):
    in_specs = (
        P("seq", "head", None),
        P("seq", "head", None),
        P("seq", "head", None),
        P(),
        P("seq", None, None),
        P("seq", None, None),
        P(),
        P(),
    )
    return jax.shard_map(
        functools.partial(per_device, mesh.shape["seq"]), mesh=mesh, in_specs=in_specs,
        out_specs=P("seq", "head", None), check_vma=False,
    )
```

```python
import functools

import jax
import jax.numpy as jnp
from jax import lax
from jax.experimental import pallas as pl
from jax.experimental.pallas import tpu as pltpu
from jax.sharding import PartitionSpec as P

BLOCK = 128
D = 128
NEG = -1e30
LOG2E = 1.4426950408889634
LOW = 1e-25
HIGH = 1e25
CHUNK = 1024


def attn_kernel(vert_ref, slash_ref, ids_ref, sink_ref, win_ref, q_ref, o0_ref, flag_ref, kv0_ref, kv1_ref, o_ref,
                kbuf, vbuf, acc, result, stamp, cnt, sem):
    heads, toks, width = q_ref.shape
    G = width // D
    blocks_here = toks // BLOCK
    first_block = lax.axis_index("seq") * blocks_here
    first_head = lax.axis_index("head") * heads
    RG = 2
    rows = RG * BLOCK
    NR = G // RG
    CB = CHUNK // BLOCK
    c2 = (D ** -0.5) * LOG2E

    def clear(i, _):
        stamp[i] = -1
        return 0
    lax.fori_loop(0, 128, clear, 0)

    def copies(kv_ref, slot, c, n):
        dst = pl.multiple_of(n * BLOCK, BLOCK)
        return (
            pltpu.make_async_copy(kv_ref.at[c, pl.ds(0, BLOCK), :], kbuf.at[slot, pl.ds(dst, BLOCK), :], sem.at[slot]),
            pltpu.make_async_copy(kv_ref.at[c, pl.ds(BLOCK, BLOCK), :], vbuf.at[slot, pl.ds(dst, BLOCK), :], sem.at[slot]),
        )

    def fetch(kv_ref, h, lb, tag):
        slot = lb
        head = first_head + h
        b = first_block + lb
        retr = (ids_ref[0] == head) | (ids_ref[1] == head) | (ids_ref[2] == head) | (ids_ref[3] == head)

        def add(c, n):
            new = stamp[c] != tag

            @pl.when(new)
            def _():
                stamp[c] = tag
                for cp in copies(kv_ref, slot, c, n):
                    cp.start()
            return n + new.astype(jnp.int32)

        def retrieval(n):
            def one(j, n):
                return add(b - slash_ref[lb, head, j], add(vert_ref[lb, head, j], n))
            return lax.fori_loop(0, 16, one, n)

        def running(n):
            n = lax.fori_loop(0, jnp.minimum(sink_ref[head], b + 1), add, n)
            return lax.fori_loop(1, jnp.minimum(win_ref[head], b + 1), lambda d, n: add(b - d, n), n)
        cnt[slot] = lax.cond(retr, retrieval, running, add(b, jnp.int32(0)))

    def arrived(kv_ref, slot):
        def one(i, _):
            for cp in copies(kv_ref, slot, 0, 0):
                cp.wait()
            return 0
        lax.fori_loop(0, cnt[slot], one, 0)
        pad = pl.ds(pl.multiple_of(cnt[slot] * BLOCK, BLOCK), BLOCK)
        kbuf[slot, pad, :] = jnp.zeros((BLOCK, D), kbuf.dtype)
        vbuf[slot, pad, :] = jnp.zeros((BLOCK, D), vbuf.dtype)

    def query_rows(h, lb, r):
        row0 = pl.multiple_of(lb * BLOCK, BLOCK)
        return jnp.concatenate([q_ref[h, pl.ds(row0, BLOCK), (r * RG + g) * D:(r * RG + g + 1) * D] for g in range(RG)], axis=0)

    def attend(h, lb, off, length, bias, first):
        kt = kbuf[lb, pl.ds(off, length), :]
        v = vbuf[lb, pl.ds(off, length), :]
        va = jnp.concatenate([v, jnp.ones_like(v)], axis=1)
        for r in range(NR):
            s = lax.dot_general(query_rows(h, lb, r), kt, (((1,), (1,)), ((), ())), preferred_element_type=jnp.float32) * c2
            if bias is not None:
                s = jnp.concatenate([s[g * BLOCK:(g + 1) * BLOCK] + bias for g in range(RG)], axis=0)
            pv = jnp.dot(jnp.exp2(s).astype(jnp.bfloat16), va, preferred_element_type=jnp.float32)
            if first:
                acc[r] = pv
            else:
                acc[r] += pv

    def fast(h, lb):
        n = cnt[lb] - 1
        col = lax.broadcasted_iota(jnp.int32, (BLOCK, BLOCK), 1)
        row = lax.broadcasted_iota(jnp.int32, (BLOCK, BLOCK), 0)
        attend(h, lb, 0, BLOCK, jnp.where(col <= row, 0.0, NEG), True)
        whole = n // CB

        def chunk(j, _):
            attend(h, lb, pl.multiple_of(BLOCK + j * CHUNK, BLOCK), CHUNK, None, False)
            return 0
        lax.fori_loop(0, whole, chunk, 0)

        half = CHUNK // 2
        halves = (n - whole * CB) // (CB // 2)

        def middle(j, _):
            attend(h, lb, pl.multiple_of(BLOCK + whole * CHUNK + j * half, BLOCK), half, None, False)
            return 0
        lax.fori_loop(0, halves, middle, 0)
        done = whole * CB + halves * (CB // 2)

        def small(j, _):
            off = pl.multiple_of(BLOCK + done * BLOCK + j * 2 * BLOCK, BLOCK)
            left = (n - done - 2 * j) * BLOCK
            col = lax.broadcasted_iota(jnp.int32, (BLOCK, 2 * BLOCK), 1)
            attend(h, lb, off, 2 * BLOCK, jnp.where(col < left, 0.0, NEG), False)
            return 0
        lax.fori_loop(0, (n - done + 1) // 2, small, 0)

    def out_of_range():
        low = acc[0, :, D:]
        high = low
        for r in range(1, NR):
            t = acc[r, :, D:]
            low, high = jnp.minimum(low, t), jnp.maximum(high, t)
        return jnp.min(jnp.where((low > LOW) & (high < HIGH), 1.0, 0.0)) < 0.5

    def careful(h, lb):
        n = cnt[lb]
        length = 2 * BLOCK
        row0 = pl.multiple_of(lb * BLOCK, BLOCK)

        def group(r, _):
            qr = jnp.concatenate([
                q_ref[h, pl.ds(row0, BLOCK), pl.ds(pl.multiple_of((r * RG + g) * D, D), D)] for g in range(RG)], axis=0)

            def chunk(j, carry):
                m, a = carry
                off = pl.multiple_of(j * length, BLOCK)
                v = vbuf[lb, pl.ds(off, length), :]
                s = lax.dot_general(qr, kbuf[lb, pl.ds(off, length), :], (((1,), (1,)), ((), ())), preferred_element_type=jnp.float32)
                col = lax.broadcasted_iota(jnp.int32, (rows, length), 1) + off
                row = lax.broadcasted_iota(jnp.int32, (rows, length), 0) % BLOCK
                s = jnp.where((col < n * BLOCK) & ((col >= BLOCK) | (col <= row)), s, NEG)
                mn = jnp.maximum(m, jnp.max(s, axis=1, keepdims=True))
                p = jnp.exp2((s - mn) * c2).astype(jnp.bfloat16)
                pv = jnp.dot(p, jnp.concatenate([v, jnp.ones_like(v)], axis=1), preferred_element_type=jnp.float32)
                return mn, a * jnp.exp2((m - mn) * c2) + pv
            zero = (jnp.full((rows, 1), NEG, jnp.float32), jnp.zeros((rows, 2 * D), jnp.float32))
            acc[r] = lax.fori_loop(0, (n + 1) // 2, chunk, zero)[1]
            return 0
        lax.fori_loop(0, NR, group, 0)

    def store(h, lb):
        row0 = pl.multiple_of(lb * BLOCK, BLOCK)
        for r in range(NR):
            o = acc[r, :, :D] / acc[r, :, D:]
            for g in range(RG):
                result[h, pl.ds(row0, BLOCK), (r * RG + g) * D:(r * RG + g + 1) * D] = o[g * BLOCK:(g + 1) * BLOCK].astype(o_ref.dtype)

    for lb in range(blocks_here):
        fetch(kv1_ref, 1, jnp.int32(lb), lb)
    result[0] = o0_ref[...]

    def head1(lb, _):
        arrived(kv1_ref, lb)
        fast(1, lb)
        bad = out_of_range()

        @pl.when(bad)
        def _():
            careful(1, lb)
        store(1, lb)
        return 0
    lax.fori_loop(0, blocks_here, head1, 0)

    def head0(lb, _):
        bad = jnp.min(flag_ref[lb]) < 0.5

        @pl.when(bad)
        def _():
            fetch(kv0_ref, 0, lb, blocks_here + lb)
            arrived(kv0_ref, lb)
            careful(0, lb)
            store(0, lb)
        return 0
    lax.fori_loop(0, blocks_here, head0, 0)
    for h in range(heads):
        o_ref[:, h, :] = result[h]


def attention(q, o0, flag, kv0, kv1, vert, slash, ids, sinks, wins):
    heads, toks, width = q.shape
    sm = pl.BlockSpec(memory_space=pltpu.SMEM)
    vm = pl.BlockSpec(memory_space=pltpu.VMEM)
    hbm = pl.BlockSpec(memory_space=pl.ANY)
    slots = 34 * BLOCK
    return pl.pallas_call(
        attn_kernel,
        out_shape=jax.ShapeDtypeStruct((toks, heads, width), jnp.bfloat16),
        in_specs=[sm] * 5 + [vm] * 3 + [hbm] * 2,
        out_specs=vm,
        scratch_shapes=[
            pltpu.VMEM((2, slots, D), jnp.bfloat16),
            pltpu.VMEM((2, slots, D), jnp.bfloat16),
            pltpu.VMEM((width // D // 2, 2 * BLOCK, 2 * D), jnp.float32),
            pltpu.VMEM((heads, toks, width), jnp.bfloat16),
            pltpu.SMEM((128,), jnp.int32),
            pltpu.SMEM((2,), jnp.int32),
            pltpu.SemaphoreType.DMA((2,)),
        ],
        compiler_params=pltpu.CompilerParams(vmem_limit_bytes=60 * 1024 * 1024),
    )(vert, slash, ids, sinks, wins, q, o0, flag, kv0, kv1)


MESH = pl.DeviceIdType.MESH
LISTED = 33
NY = 4
NZ = 8


def gather_plan(ny, nz, layers, a_rows, b_rows, starts):
    half = {"A": a_rows // 2, "B": b_rows // 2}
    base = {"A": 0, "B": a_rows}
    first = {"A": "z", "B": "y"}
    second = {"A": "y", "B": "z"}
    length = {"y": ny, "z": nz}
    latency, rate, near = 2.0, 46.5e3 / 512.0, 300e3 / 512.0

    def rows(part, sub):
        if part == "W":
            return 0, a_rows + b_rows
        if sub == 0:
            return base[part], 2 * half[part]
        return base[part] + (sub - 1) * half[part], half[part]

    free, halves, whole = {}, {}, {}
    heap = []
    count = [0]
    order = []

    def push(time, what):
        count[0] += 1
        heap.append((time, count[0], what))

    def send(layer, part, sub, off, axis, way, now, sends):
        n = rows(part, sub)[1]
        begin = max(now, free.get((axis, way), 0.0))
        share = near if axis == "c" else 2.0 * rate * (length[axis] // 2 - (way < 0)) / (length[axis] - 1)
        end = begin + n / share
        free[(axis, way)] = end
        sends.append((layer, part, sub, off, axis, way))
        dy, dz = off
        if axis == "z":
            dz = (dz - way) % nz
        if axis == "y":
            dy = (dy - way) % ny
        push(end + (1.0 if axis == "c" else latency), (layer, part, sub, (dy, dz), axis, way))

    def complete(layer, part, off, axis, now, sends):
        whole[(layer, off)] = whole.get((layer, off), 0) + 1
        if whole[(layer, off)] == 2:
            send(layer, "W", 0, off, "c", 0, now, sends)
        if axis == first[part]:
            for way in (1, -1):
                send(layer, part, 0, off, second[part], way, now, sends)

    for layer in range(layers):
        push(starts[layer], (layer, None))
    while heap:
        heap.sort(key=lambda e: e[:2])
        now, _, what = heap.pop(0)
        sends = []
        if what[1] is None:
            layer = what[0]
            for part in ("B", "A"):
                for way in (1, -1):
                    send(layer, part, 0, (0, 0), first[part], way, now, sends)
            for part in ("A", "B"):
                for way in (1, -1):
                    send(layer, part, 0, (0, 0), second[part], way, now, sends)
            send(layer, "W", 0, (0, 0), "c", 0, now, sends)
            order.append((now, what, sends))
            continue
        layer, part, sub, off, axis, way = what
        if axis != "c":
            n = length[axis]
            dist = (-way * (off[1] if axis == "z" else off[0])) % n
            if dist < n // 2 - (way < 0):
                send(layer, part, 0, off, axis, way, now, sends)
            complete(layer, part, off, axis, now, sends)
        order.append((now, what, sends))
    return order, rows


def gather_kernel(a_rows, start1, unit_us, vert_ref, slash_ref, ids_ref, sink_ref, win_ref, q_ref, k_ref, v_ref,
                  kv0_out, kv1_out, qt_out, o_ref, flag_ref,
                  kv0, shard, qt, acc, cand, usable, send_sem, whole_sem, recv_sem, local_sem):
    ny, nz = NY, NZ
    me = lax.axis_index("seq")
    head_slot = lax.axis_index("head")
    toks, heads, width = q_ref.shape
    dim = k_ref.shape[2]
    G = width // dim
    blocks_here = toks // BLOCK
    y, z, core = me // (2 * nz), lax.rem(me // 2, nz), lax.rem(me, 2)
    turn = 1 - 2 * core
    order, rows = gather_plan(ny, nz, 2, a_rows, 2 * BLOCK - a_rows, (0.0, start1))
    c2 = (dim ** -0.5) * LOG2E

    for h in range(heads):
        for lb in range(blocks_here):
            shard[h, lb, :BLOCK, :] = k_ref[lb * BLOCK:(lb + 1) * BLOCK, h, :]
            shard[h, lb, BLOCK:, :] = v_ref[lb * BLOCK:(lb + 1) * BLOCK, h, :]

    def seq_of(dy, dz, c):
        return (lax.rem(y + turn * dy + ny, ny) * nz + lax.rem(z + turn * dz + nz, nz)) * 2 + c

    target = {
        ("y", 1): seq_of(1, 0, core), ("y", -1): seq_of(ny - 1, 0, core),
        ("z", 1): seq_of(0, 1, core), ("z", -1): seq_of(0, nz - 1, core),
        ("c", 0): seq_of(0, 0, 1 - core),
    }
    barrier = pltpu.get_barrier_semaphore()
    for t in target.values():
        pl.semaphore_signal(barrier, inc=1, device_id={"seq": t}, device_id_type=MESH)
    pl.semaphore_wait(barrier, len(target))

    held = (kv0, kv1_out)

    def blocks_of(seq):
        return pl.ds(seq * blocks_here, blocks_here)
    own = [pltpu.make_async_copy(shard.at[layer], held[layer].at[blocks_of(me)], local_sem.at[layer]) for layer in range(2)]
    for copy in own:
        copy.start()
    recv_id = {}

    def number(key):
        return recv_id.setdefault(key, len(recv_id))

    def piece(layer, part, sub, off, axis, way):
        dy, dz = off
        to = (dy, (dz - way) % nz) if axis == "z" else ((dy - way) % ny, dz) if axis == "y" else off
        lo, n = rows(part, sub)
        place = held[layer].at[blocks_of(seq_of(dy, dz, core)), pl.ds(lo, n), :]
        source = shard.at[layer, :, pl.ds(lo, n), :] if off == (0, 0) else place
        copy = pltpu.make_async_remote_copy(
            src_ref=source, dst_ref=place,
            send_sem=send_sem.at[layer],
            recv_sem=whole_sem.at[layer] if axis == "c" else recv_sem.at[number((layer, part, sub, to))],
            device_id={"seq": target[(axis, way)]}, device_id_type=MESH,
        )
        return copy

    def arrive(what):
        layer, part, sub, off, _, _ = what
        lo, n = rows(part, sub)
        place = held[layer].at[blocks_of(seq_of(off[0], off[1], core)), pl.ds(lo, n), :]
        pltpu.make_async_copy(place, place, recv_sem.at[number((layer, part, sub, off))]).wait()

    def await_bytes(layer, blocks, sem):
        place = held[layer].at[pl.ds(0, blocks)]
        pltpu.make_async_copy(place, place, sem.at[layer]).wait()

    def handle(event):
        _, what, sends = event
        if what[1] not in (None, "W"):
            arrive(what)
        for s in sends:
            piece(*s).start()

    head0 = head_slot * heads

    def one_if(condition):
        return condition.astype(jnp.int32)
    hits = one_if(ids_ref[0] == head0) + one_if(ids_ref[1] == head0) + one_if(ids_ref[2] == head0) + one_if(ids_ref[3] == head0)
    retr = one_if(hits > 0)

    def list_blocks(lb):
        b = me * blocks_here + lb
        sinks, wins = sink_ref[head0], win_ref[head0]
        at = lb * 64
        cand[at] = b
        usable[at] = 1
        for j in range(1, LISTED):
            listed = vert_ref[lb, head0, j - 1] if j <= 16 else b - slash_ref[lb, head0, j - 17]
            if j <= 2:
                read = j - 1
                ok = one_if(j - 1 < sinks) * one_if(j - 1 <= b)
            elif j <= 6:
                read = b - (j - 2)
                ok = one_if(j - 2 < wins) * one_if(j - 2 <= b)
            else:
                read, ok = -1 - j, 0
            ok = retr + (1 - retr) * ok
            cand[at + j] = ok * (retr * listed + (1 - retr) * read) - (1 - ok) * (1 + j)

        def mark(j, _):
            mine = cand[at + j]
            same = 0
            for k in range(LISTED):
                same = same + one_if(k < j) * one_if(cand[at + k] == mine)
            usable[at + j] = one_if(mine >= 0) * one_if(same == 0)
            return 0
        lax.fori_loop(1, LISTED, mark, 0)

    def query_rows(lb, r):
        return jnp.concatenate([qt[0, lb * BLOCK:(lb + 1) * BLOCK, (2 * r + g) * dim:(2 * r + g + 1) * dim] for g in range(2)], axis=0)

    def attend(lb, kt, va, bias):
        for r in range(G // 2):
            s = lax.dot_general(query_rows(lb, r), kt, (((1,), (1,)), ((), ())), preferred_element_type=jnp.float32) * c2
            if bias is not None:
                s = jnp.concatenate([s[:BLOCK] + bias, s[BLOCK:] + bias], axis=0)
            pv = jnp.dot(jnp.exp2(s).astype(jnp.bfloat16), va, preferred_element_type=jnp.float32)
            if bias is not None:
                acc[r] = pv
            else:
                acc[r] += pv

    def diagonal(lb):
        kt = shard[0, lb, :BLOCK, :]
        v = shard[0, lb, BLOCK:, :]
        col = lax.broadcasted_iota(jnp.int32, (BLOCK, BLOCK), 1)
        row = lax.broadcasted_iota(jnp.int32, (BLOCK, BLOCK), 0)
        attend(lb, kt, jnp.concatenate([v, jnp.ones_like(v)], axis=1), jnp.where(col <= row, 0.0, NEG))

    def listed_blocks(lb, j0, count):
        ks, vs = [], []
        for j in range(count):
            c = jnp.minimum(jnp.maximum(cand[lb * 64 + j0 + j], 0), kv0.shape[0] - 1)
            weight = usable[lb * 64 + j0 + j].astype(jnp.float32)
            weights = jnp.full((BLOCK, dim), weight, jnp.float32).astype(jnp.bfloat16)
            ks.append(kv0[c, :BLOCK, :])
            vs.append(jnp.concatenate([kv0[c, BLOCK:, :] * weights, weights], axis=1))
        attend(lb, jnp.concatenate(ks, axis=0), jnp.concatenate(vs, axis=0), None)

    def finish(lb):
        low = acc[0, :, dim:]
        high = low
        for r in range(G // 2):
            t = acc[r, :, dim:]
            o = acc[r, :, :dim] / t
            low, high = jnp.minimum(low, t), jnp.maximum(high, t)
            for g in range(2):
                o_ref[lb * BLOCK:(lb + 1) * BLOCK, (2 * r + g) * dim:(2 * r + g + 1) * dim] = o[g * BLOCK:(g + 1) * BLOCK].astype(o_ref.dtype)
        flag_ref[lb] = jnp.where((low > LOW) & (high < HIGH), 1.0, 0.0)

    span = 8
    units = []
    for lb in range(blocks_here):
        units.append(functools.partial(diagonal, lb))
        for j0 in range(1, LISTED, span):
            units.append(functools.partial(listed_blocks, lb, j0, span))
        units.append(functools.partial(finish, lb))
    spare = [functools.partial(list_blocks, lb) for lb in range(blocks_here)]

    def split_queries(i):
        for h in range(heads):
            qt[h, i * 64:(i + 1) * 64, :] = q_ref[i * 64:(i + 1) * 64, h, :]
    spare += [functools.partial(split_queries, i) for i in range(toks // 64)]

    last0 = max(i for i, e in enumerate(order) if e[1][0] == 0)
    tail = []
    own[0].wait()
    for i, event in enumerate(order[:last0 + 1]):
        handle(event)
        if i % 8 == 2 and spare:
            spare.pop(0)()
    for work in spare:
        work()
    total = kv0.shape[0]
    await_bytes(0, total // 2, whole_sem)
    keep = pltpu.make_async_copy(kv0, kv0_out, local_sem.at[2])
    keep.start()
    keep_q = pltpu.make_async_copy(qt, qt_out, local_sem.at[3])
    keep_q.start()
    rest = order[last0 + 1:]
    clock = order[last0][0]
    for work in units:
        while rest and rest[0][0] <= clock:
            handle(rest.pop(0))
        work()
        if work.func is listed_blocks:
            clock += unit_us
    for event in rest:
        handle(event)
    await_bytes(1, total // 2, whole_sem)
    for layer in range(2):
        await_bytes(layer, total - blocks_here, send_sem)
    own[1].wait()
    keep.wait()
    keep_q.wait()


def gather(queries, keys, values, vert, slash, ids, sinks, wins, n_seq, a_rows=160, start1=14.0, unit_us=1.7):
    toks, heads, width = queries.shape
    dim = keys.shape[2]
    order, _ = gather_plan(NY, NZ, 2, a_rows, 2 * BLOCK - a_rows, (0.0, start1))
    arrivals = sum(e[1][1] not in (None, "W") for e in order)
    sm = pl.BlockSpec(memory_space=pltpu.SMEM)
    vm = pl.BlockSpec(memory_space=pltpu.VMEM)
    hbm = pl.BlockSpec(memory_space=pl.ANY)
    bf = jnp.bfloat16
    return pl.pallas_call(
        functools.partial(gather_kernel, a_rows, start1, unit_us),
        out_shape=(
            jax.ShapeDtypeStruct((n_seq * toks // BLOCK, 2 * BLOCK, dim), bf),
            jax.ShapeDtypeStruct((n_seq * toks // BLOCK, 2 * BLOCK, dim), bf),
            jax.ShapeDtypeStruct((heads, toks, width), bf),
            jax.ShapeDtypeStruct((toks, width), bf),
            jax.ShapeDtypeStruct((toks // BLOCK, 2 * BLOCK, dim), jnp.float32),
        ),
        in_specs=[sm] * 5 + [vm] * 3,
        out_specs=(hbm, hbm, hbm, vm, vm),
        scratch_shapes=[
            pltpu.VMEM((n_seq * toks // BLOCK, 2 * BLOCK, dim), bf),
            pltpu.VMEM((heads, toks // BLOCK, 2 * BLOCK, dim), bf),
            pltpu.VMEM((heads, toks, width), bf),
            pltpu.VMEM((width // dim // 2, 2 * BLOCK, 2 * dim), jnp.float32),
            pltpu.SMEM((toks // BLOCK * 64,), jnp.int32),
            pltpu.SMEM((toks // BLOCK * 64,), jnp.int32),
            pltpu.SemaphoreType.DMA((2,)),
            pltpu.SemaphoreType.DMA((2,)),
            pltpu.SemaphoreType.DMA((arrivals,)),
            pltpu.SemaphoreType.DMA((4,)),
        ],
        compiler_params=pltpu.CompilerParams(
            collective_id=0, has_side_effects=True, vmem_limit_bytes=60 * 1024 * 1024,
        ),
    )(vert, slash, ids, sinks, wins, queries, keys, values)


def per_device(
    n_seq, queries, keys, values, retrieval_ids, vertical_blocks, slash_offsets, sink_blocks, window_blocks
):
    lists = (vertical_blocks, slash_offsets, retrieval_ids, sink_blocks, window_blocks)
    kv0, kv1, q, o0, flag = gather(queries, keys, values, *lists, n_seq)
    return attention(q, o0, flag, kv0, kv1, *lists)


def solution(mesh):
    in_specs = (
        P("seq", "head", None),
        P("seq", "head", None),
        P("seq", "head", None),
        P(),
        P("seq", None, None),
        P("seq", None, None),
        P(),
        P(),
    )
    return jax.shard_map(
        functools.partial(per_device, mesh.shape["seq"]), mesh=mesh, in_specs=in_specs,
        out_specs=P("seq", "head", None), check_vma=False,
    )
```
